128 devices in a mesh: row: 16 (over x, z), col: 8 (over y, core).
Axes of the slice: x: 4, y: 4, z: 4, core: 2. Of those that a mesh axis runs over, the one named last changes fastest.
Arguments:
- child_tiles: float32 [1024, 256, 256], P(('row', 'col')), may hold values from -2 to 2
- tile_dest: int32 [1024, 2], P(('row', 'col')), may hold values from 0 to 31, as said below
- tile_counts: int32 [16, 8], P('row', 'col'), may hold values from 4 to 8
- child_offsets: int32 [4], replicated, may hold values from 0 to 16
Outputs:
- r_top: float32 [1024, 8192], P(None, 'col')
The draws below stay inside these ranges and needn't reach their ends.
Inputs may be any that keep to these rules, and one draw needn't show every extreme that they name: tile_dest[t, 0] is a column tile of the front and tile_dest[t, 1] is below 7. Among the 8 slots of one count entry, at most 2 name column tiles of one block of 4 consecutive column tiles (blocks start at multiples of 4); some entry reaches 2 for some block, and some block receives 2 live slots from every entry that shares a row offset residue.
All inputs are finite; a program needn't handle non-finite values.
Results may differ from the reference program's by a relative error of at most 0.00008.
Values sent between devices are 32-bit elements; how exact they have to be, the bound alone decides.
No kernel may reach another device: no remote copies, remote signals or barrier semaphores. Data moves between devices by JAX's collectives and lax.ppermute only.
A program may use at most 128 MiB of HBM per device.

```python
import jax
import jax.numpy as jnp
from jax import lax

NB = 256
NC = 8192
PANELS = 4
CHILDREN = 4
SLOTS = 8
CAPC = 2
COUNT_ROWS = 16
COUNT_COLS = 8
RT = 128
KB = 7
CTD = 4
TILE_SLOTS = 1024


def shared_center(key):
    sub_key = jax.random.fold_in(key, 7919)
    first_key, second_key, third_key = jax.random.split(sub_key, 3)
    center_row = jax.random.randint(first_key, (), 0, COUNT_ROWS)
    center_col = jax.random.randint(second_key, (), 0, COUNT_COLS)
    offsets = jax.random.randint(third_key, (CHILDREN,), 0, COUNT_ROWS + 1)
    pick_key, other_key = jax.random.split(jax.random.fold_in(sub_key, 4409))
    top_child = jax.random.randint(pick_key, (), 0, CHILDREN)
    low_child = (top_child + 1 + jax.random.randint(other_key, (), 0, CHILDREN - 1)) % CHILDREN
    child_ids = jnp.arange(CHILDREN)
    offsets = jnp.where(child_ids == top_child, COUNT_ROWS, offsets)
    offsets = jnp.where(child_ids == low_child, 0, offsets)
    return (center_row, center_col, offsets)


def center_devices(key):
    center_row, center_col, offsets = shared_center(key)
    device_ids = jnp.arange(COUNT_ROWS * COUNT_COLS)
    row_ids = device_ids // COUNT_COLS
    col_ids = device_ids % COUNT_COLS
    child_ids = col_ids // (COUNT_COLS // CHILDREN)
    arrive_row = (offsets[child_ids] + row_ids) % COUNT_ROWS
    return (arrive_row == center_row, center_col)


def draw_child_offsets(key, part):
    center_row, center_col, offsets = shared_center(key)
    return offsets.astype(jnp.int32)


def draw_tile_counts(key, part):
    is_center, center_col = center_devices(key)
    sub_key = jax.random.fold_in(key, 31)
    counts = jax.random.randint(sub_key, (COUNT_ROWS * COUNT_COLS,), SLOTS // 2, SLOTS + 1)
    counts = jnp.where(is_center, SLOTS, counts)
    return counts.reshape(COUNT_ROWS, COUNT_COLS).astype(jnp.int32)


def draw_tile_dest(key, part):
    is_center, center_col = center_devices(key)
    total = COUNT_ROWS * COUNT_COLS
    entries = COUNT_COLS * CAPC
    device_keys = jax.random.split(jax.random.fold_in(key, 57), total)

    def one_device(device_key, center_flag):
        key_a, key_b, key_c, key_d, key_e = jax.random.split(device_key, 5)
        forced = jax.random.randint(key_a, (), 0, COUNT_COLS)
        forced = jnp.where(center_flag, center_col, forced)
        scores = jax.random.permutation(key_b, entries).astype(jnp.int32)
        owners = jnp.arange(entries, dtype=jnp.int32) // CAPC
        scores = jnp.where(owners == forced, scores - entries, scores)
        chosen = jnp.argsort(scores, stable=True)[:SLOTS]
        chosen = jax.random.permutation(key_c, chosen)
        owner_cols = chosen // CAPC
        col_tiles = owner_cols * CTD + jax.random.randint(key_d, (SLOTS,), 0, CTD)
        blocks = jax.random.randint(key_e, (SLOTS,), 0, KB)
        return jnp.stack([col_tiles, blocks], axis=1).astype(jnp.int32)
    result = jax.vmap(one_device)(device_keys, is_center)
    return result.reshape(total * SLOTS, 2)


def block_scale(stream_key, shape, cuts, low, top_value):
    loudness = 1.0
    for axis_at, blocks in cuts:
        heights = jax.random.uniform(jax.random.fold_in(jax.random.fold_in(stream_key, 6), axis_at), (blocks,), jnp.float32, low / len(cuts), top_value / len(cuts))
        loudness = loudness * jnp.repeat(jnp.exp(heights), shape[axis_at] // blocks).reshape((-1,) + (1,) * (len(shape) - 1 - axis_at))
    return loudness


def scatter_about(stream_key, shape, scale, most, pieces=(), kind=jnp.bfloat16):
    factor_of = block_scale(stream_key, shape, pieces, -0.22, 0.18) if pieces else 1.0
    values = jax.random.normal(stream_key, shape, jnp.float32) * scale * factor_of
    return jnp.minimum(jnp.maximum(values, -most), most).astype(kind)


def setup_inputs(seed: int = 0) -> dict:
    keys = jax.random.split(jax.random.key(seed), 5)
    child_tiles = scatter_about(keys[0], (TILE_SLOTS, NB, NB), 0.25, 2.0, ((0, 128),), jnp.float32)
    tile_dest = draw_tile_dest(jax.random.fold_in(keys[4], 71), 0)
    tile_counts = draw_tile_counts(jax.random.fold_in(keys[4], 71), 0)
    child_offsets = draw_child_offsets(jax.random.fold_in(keys[4], 71), 0)
    return {"child_tiles": child_tiles, "tile_dest": tile_dest, "tile_counts": tile_counts, "child_offsets": child_offsets}


def reference(child_tiles, tile_dest, tile_counts, child_offsets):
    per_child = COUNT_COLS // CHILDREN
    front = jnp.zeros((RT * NB, NC), jnp.float32)

    def place_tile(slot_index, front):
        slot_index = jnp.asarray(slot_index).astype(jnp.int32)
        device_index = slot_index // SLOTS
        slot_pos = slot_index % SLOTS
        row_pos = device_index // COUNT_COLS
        col_pos = device_index % COUNT_COLS
        is_live = slot_pos < tile_counts[row_pos, col_pos]
        child_pos = col_pos // per_child
        row_tile = child_offsets[child_pos] + row_pos + COUNT_ROWS * tile_dest[slot_index, 1]
        col_tile = tile_dest[slot_index, 0]
        start_row = (row_tile * NB).astype(jnp.int32)
        start_col = (col_tile * NB).astype(jnp.int32)
        old_tile = lax.dynamic_slice(front, (start_row, start_col), (NB, NB))
        new_tile = old_tile + jnp.where(is_live, child_tiles[slot_index], jnp.zeros_like(old_tile))
        return lax.dynamic_update_slice(front, new_tile, (start_row, start_col))
    front = lax.fori_loop(0, COUNT_ROWS * COUNT_COLS * SLOTS, place_tile, front)
    width = PANELS * NB
    leading = front[:, :width]
    gram_block = jnp.dot(leading.T.astype(jnp.float32), leading.astype(jnp.float32), precision=lax.Precision.HIGHEST, preferred_element_type=jnp.float32)
    cross_terms = jnp.dot(leading.T.astype(jnp.float32), front.astype(jnp.float32), precision=lax.Precision.HIGHEST, preferred_element_type=jnp.float32)
    lower_factor = jnp.linalg.cholesky(gram_block)
    rows_out = jax.scipy.linalg.solve_triangular(lower_factor, cross_terms, lower=True)
    upper_mask = jnp.arange(NC)[None, :] >= jnp.arange(width)[:, None]
    return jnp.where(upper_mask, rows_out, jnp.zeros_like(rows_out))
```

```python
import jax
import jax.numpy as jnp
from jax import lax
from jax.experimental import pallas as pl
from jax.experimental.pallas import tpu as pltpu
from jax.sharding import PartitionSpec as P

NC = 8192
PANELS = 4
CHILDREN = 4
CAPC = 2
RTD = 8
BLK = 128
GRAM_SLOTS = 5
CHUNKS = 1
HIGHEST = lax.Precision.HIGHEST
F32 = jnp.float32
BF16 = jnp.bfloat16
VMEM_LIMIT = 56 << 20


def split(x):
    high = x.astype(BF16)
    return high, (x - high.astype(F32)).astype(BF16)


def dot3(a_high, a_low, b_high, b_low):
    left = jnp.concatenate([a_high, a_high, a_low], axis=1)
    right = jnp.concatenate([b_high, b_low, b_high], axis=0)
    return jnp.dot(left, right, preferred_element_type=F32)


def params():
    return pltpu.CompilerParams(vmem_limit_bytes=VMEM_LIMIT)


def take_tiles(tiles, picks):
    count, (high, wide) = picks.shape[0], tiles.shape[1:]

    def kernel(pick_ref, in_ref, out_ref):
        out_ref[...] = in_ref[...]

    return pl.pallas_call(
        kernel,
        grid_spec=pltpu.PrefetchScalarGridSpec(
            num_scalar_prefetch=1,
            grid=(count,),
            in_specs=[pl.BlockSpec((1, high, wide), lambda i, pick: (pick[i], 0, 0))],
            out_specs=pl.BlockSpec((1, high, wide), lambda i, pick: (i, 0, 0)),
        ),
        out_shape=jax.ShapeDtypeStruct((count, high, wide), F32),
        cost_estimate=pl.CostEstimate(flops=0, bytes_accessed=8 * count * high * wide, transcendentals=0),
        name="take_tiles",
    )(picks, tiles)


def gram_table(col_count):
    blocks = col_count
    table = []
    for c in range(col_count):
        low = min(c, blocks - 1 - c)
        shared = [(i, j) for i in (low, blocks - 1 - low) for j in range(i, blocks)]
        mine = shared[::2] if c == low else shared[1::2]
        table.append((mine + mine[-1:])[: GRAM_SLOTS])
    return table


def place_leads(pos_ref, lead_refs, sum_ref, transposed):
    sum_ref[...] = jnp.zeros_like(sum_ref)
    count, size = lead_refs[0].shape[:2]
    for s, ref in enumerate(lead_refs):

        def place(r, _, s=s, ref=ref):
            pos = pos_ref[s * count + r]

            @pl.when(pos >= 0)
            def _():
                at_row = pl.ds(pl.multiple_of((pos // PANELS) * size, size), size)
                at_col = pl.ds(pl.multiple_of((pos % PANELS) * size, size), size)
                if transposed:
                    sum_ref[at_col, at_row] += ref[r].T
                else:
                    sum_ref[at_row, at_col] += ref[r]

            return 0

        lax.fori_loop(0, count, place, 0)


def gram_slice(mine, positions, leads):
    size = leads[0].shape[1]
    width, depth = PANELS * size, RTD * size

    def kernel(mine_ref, pos_ref, *refs):
        lead_refs, (out_ref, sum_ref, left_ref) = refs[: len(leads)], refs[len(leads) :]
        place_leads(pos_ref, lead_refs, sum_ref, False)

        def block(s, _):
            at_i = pl.ds(pl.multiple_of(mine_ref[2 * s] * BLK, BLK), BLK)
            at_j = pl.ds(pl.multiple_of(mine_ref[2 * s + 1] * BLK, BLK), BLK)
            at_s = pl.ds(pl.multiple_of(s * BLK, BLK), BLK)
            for k in range(RTD):
                rows = slice(k * size, (k + 1) * size)
                left_ref[:, rows] = sum_ref[rows, at_i].T
            a_high, a_low = split(left_ref[...])
            b_high, b_low = split(sum_ref[:, at_j])
            block_out = dot3(a_high, a_low, b_high, b_low)
            for g in range(BLK // 8):
                out_ref[g, :, at_s] = block_out[8 * g : 8 * g + 8]
            return 0

        lax.fori_loop(0, GRAM_SLOTS, block, 0)

    smem = pl.BlockSpec(memory_space=pltpu.SMEM)
    vmem = pl.BlockSpec(memory_space=pltpu.VMEM)
    return pl.pallas_call(
        kernel,
        in_specs=[smem, smem] + [vmem] * len(leads),
        out_specs=vmem,
        out_shape=jax.ShapeDtypeStruct((BLK // 8, 8, GRAM_SLOTS * BLK), F32),
        scratch_shapes=[pltpu.VMEM((depth, width), F32), pltpu.VMEM((BLK, depth), F32)],
        compiler_params=params(),
        cost_estimate=pl.CostEstimate(
            flops=6 * BLK * width * depth, bytes_accessed=4 * 16 * size * size, transcendentals=0
        ),
        name="gram_slice",
    )(mine, positions, *leads)


def leading_split(positions, leads):
    size = leads[0].shape[1]
    width, depth = PANELS * size, RTD * size

    def kernel(pos_ref, *refs):
        lead_refs, (high_ref, low_ref, sum_ref) = refs[: len(leads)], refs[len(leads) :]
        place_leads(pos_ref, lead_refs, sum_ref, True)

        def step(k, _):
            rows = pl.ds(pl.multiple_of(k * BLK, BLK), BLK)
            high_ref[rows, :], low_ref[rows, :] = split(sum_ref[rows, :])
            return 0

        lax.fori_loop(0, width // BLK, step, 0)

    smem = pl.BlockSpec(memory_space=pltpu.SMEM)
    vmem = pl.BlockSpec(memory_space=pltpu.VMEM)
    return pl.pallas_call(
        kernel,
        in_specs=[smem] + [vmem] * len(leads),
        out_specs=[vmem, vmem],
        out_shape=[jax.ShapeDtypeStruct((width, depth), BF16)] * 2,
        scratch_shapes=[pltpu.VMEM((width, depth), F32)],
        compiler_params=params(),
        cost_estimate=pl.CostEstimate(flops=0, bytes_accessed=12 << 20, transcendentals=0),
        name="leading_split",
    )(positions, *leads)


def cross_products(positions, tiles, lead_high, lead_low):
    size, wide = tiles.shape[1:]
    width, depth = lead_high.shape
    cols = PANELS * wide

    def kernel(pos_ref, tile_ref, high_ref, low_ref, out_ref):
        i = pl.program_id(0)

        @pl.when(i == 0)
        def _():
            out_ref[...] = jnp.zeros_like(out_ref)

        pos = pos_ref[i]

        @pl.when(pos >= 0)
        def _():
            at_row = pl.ds(pl.multiple_of((pos // PANELS) * size, size), size)
            at_col = pl.ds(pl.multiple_of((pos % PANELS) * wide, wide), wide)
            b_high, b_low = split(tile_ref[0])
            out_ref[:, at_col] += dot3(high_ref[:, at_row], low_ref[:, at_row], b_high, b_low)

    count = tiles.shape[0]
    return pl.pallas_call(
        kernel,
        grid_spec=pltpu.PrefetchScalarGridSpec(
            num_scalar_prefetch=1,
            grid=(count,),
            in_specs=[
                pl.BlockSpec((1, size, wide), lambda i, pos: (i, 0, 0)),
                pl.BlockSpec((width, depth), lambda i, pos: (0, 0), pipeline_mode=pl.Buffered(1)),
                pl.BlockSpec((width, depth), lambda i, pos: (0, 0), pipeline_mode=pl.Buffered(1)),
            ],
            out_specs=pl.BlockSpec((width, cols), lambda i, pos: (0, 0)),
        ),
        out_shape=jax.ShapeDtypeStruct((width, cols), F32),
        compiler_params=params(),
        cost_estimate=pl.CostEstimate(
            flops=6 * count * width * size * wide, bytes_accessed=16 << 20, transcendentals=0
        ),
        name="cross_products",
    )(positions, tiles, lead_high, lead_low)


def block_factor(block):
    tiles = BLK // 8
    lane = lax.broadcasted_iota(jnp.int32, (8, BLK), 1)
    sub = lax.broadcasted_iota(jnp.int32, (8, BLK), 0)
    full = lambda v: jnp.broadcast_to(v, (8, BLK))
    x = [block[8 * t : 8 * t + 8, :] for t in range(tiles)]
    out = []
    for t in range(tiles):
        base = 8 * t
        panel = lane // 8 == t
        rows = [full(x[t][p : p + 1, :]) for p in range(8)]
        a = {(p, q): full(rows[p][:, base + q : base + q + 1]) for p in range(8) for q in range(p, 8)}
        rows = [jnp.where(panel, jnp.where(lane == base + p, 1.0, 0.0), rows[p]) for p in range(8)]
        columns = {u: [full(x[u][:, base + p : base + p + 1]) for p in range(8)] for u in range(t + 1, tiles)}
        for u in range(t + 1, tiles):
            x[u] = jnp.where(panel, 0.0, x[u])
        scales = []
        for p in range(8):
            inverse = 1.0 / a[p, p]
            scale = lax.rsqrt(a[p, p])
            scales.append(scale * (1.5 - 0.5 * a[p, p] * scale * scale))
            scaled = rows[p] * inverse
            ratio = [a[p, q] * inverse for q in range(p + 1, 8)]
            for q in range(p + 1, 8):
                for r in range(q, 8):
                    a[q, r] = a[q, r] - a[p, q] * ratio[r - p - 1]
                rows[q] = rows[q] - a[p, q] * scaled
            for u in range(t + 1, tiles):
                for q in range(p + 1, 8):
                    columns[u][q] = columns[u][q] - columns[u][p] * ratio[q - p - 1]
                x[u] = x[u] - columns[u][p] * scaled
        tile = rows[0] * scales[0]
        for p in range(1, 8):
            tile = jnp.where(sub == p, rows[p] * scales[p], tile)
        out.append(jnp.where(lane <= sub + base, tile, 0.0))
    return jnp.concatenate(out, axis=0)


def inverse_cholesky(spots, parts, width):
    blocks = width // BLK

    def kernel(spot_ref, *refs):
        part_refs, (out_ref, work_ref, row_ref) = refs[: len(parts)], refs[len(parts) :]
        for n, ref in enumerate(part_refs):
            count = ref.shape[0]

            def fill(s, _, n=n, ref=ref, count=count):
                q, r = s // GRAM_SLOTS, s % GRAM_SLOTS
                at = 2 * (n * count * GRAM_SLOTS + s)
                row = pl.multiple_of(spot_ref[at] * BLK, BLK)
                col = pl.multiple_of(spot_ref[at + 1] * BLK, BLK)
                lanes = pl.ds(pl.multiple_of(r * BLK, BLK), BLK)
                for g in range(BLK // 8):
                    work_ref[pl.ds(row + 8 * g, 8), pl.ds(col, BLK)] = ref[q, g, :, lanes]
                return 0

            lax.fori_loop(0, count * GRAM_SLOTS, fill, 0)

        def outer(k, _):
            at = pl.multiple_of(k * BLK, BLK)
            here = pl.ds(at, BLK)
            inverse = block_factor(work_ref[here, here])

            def clear(i, _):
                work_ref[pl.ds(pl.multiple_of(i * BLK, BLK), BLK), here] = jnp.zeros((BLK, BLK), F32)
                return 0

            row_ref[...] = jnp.dot(inverse, work_ref[here, :], precision=HIGHEST, preferred_element_type=F32)
            row_ref[:, here] = inverse
            lax.fori_loop(k + 1, blocks, clear, 0)
            row = row_ref[...]
            lane = lax.broadcasted_iota(jnp.int32, (BLK, width), 1)
            out_ref[here, :] = jnp.where(lane < at + BLK, row, 0.0)

            def inner(i, _):
                below = pl.ds(pl.multiple_of(i * BLK, BLK), BLK)
                factor = row_ref[:, below].T
                work_ref[below, :] -= jnp.dot(factor, row, precision=HIGHEST, preferred_element_type=F32)
                return 0

            lax.fori_loop(k + 1, blocks, inner, 0)
            return 0

        lax.fori_loop(0, blocks, outer, 0)

    smem = pl.BlockSpec(memory_space=pltpu.SMEM)
    vmem = pl.BlockSpec(memory_space=pltpu.VMEM)
    return pl.pallas_call(
        kernel,
        in_specs=[smem] + [vmem] * len(parts),
        out_specs=vmem,
        out_shape=jax.ShapeDtypeStruct((width, width), F32),
        scratch_shapes=[pltpu.VMEM((width, width), F32), pltpu.VMEM((BLK, width), F32)],
        compiler_params=params(),
        cost_estimate=pl.CostEstimate(flops=60 << 30, bytes_accessed=8 << 20, transcendentals=0),
        name="inverse_cholesky",
    )(spots, *parts)


def solved_rows(col_here, inverse, crosses):
    width, cols = crosses[0].shape[0], sum(c.shape[1] for c in crosses)
    wide = crosses[0].shape[1] // PANELS
    size = wide * len(crosses)

    def kernel(col_ref, inv_ref, *refs):
        cross_refs, (out_ref, high_ref, low_ref) = refs[: len(crosses)], refs[len(crosses) :]
        i = pl.program_id(0)

        @pl.when(i == 0)
        def _():
            high_ref[...], low_ref[...] = split(inv_ref[...])

        b_high, b_low = split(jnp.concatenate([ref[...] for ref in cross_refs], axis=1))
        first = col_ref[0] * cols + i * size
        step = 256
        for k in range(width // step):
            rows, done = slice(k * step, (k + 1) * step), (k + 1) * step
            value = dot3(high_ref[rows, :done], low_ref[rows, :done], b_high[:done], b_low[:done])
            row = lax.broadcasted_iota(jnp.int32, (step, size), 0) + k * step
            col = lax.broadcasted_iota(jnp.int32, (step, size), 1) + first
            out_ref[rows, :] = jnp.where(col >= row, value, 0.0)

    return pl.pallas_call(
        kernel,
        grid_spec=pltpu.PrefetchScalarGridSpec(
            num_scalar_prefetch=1,
            grid=(cols // size,),
            in_specs=[pl.BlockSpec((width, width), lambda i, col: (0, 0), pipeline_mode=pl.Buffered(1))]
            + [pl.BlockSpec((width, wide), lambda i, col: (0, i))] * len(crosses),
            out_specs=pl.BlockSpec((width, size), lambda i, col: (0, i)),
            scratch_shapes=[pltpu.VMEM((width, width), BF16)] * 2,
        ),
        out_shape=jax.ShapeDtypeStruct((width, cols), F32),
        compiler_params=params(),
        cost_estimate=pl.CostEstimate(flops=6 * width * width * cols, bytes_accessed=12 << 20, transcendentals=0),
        name="solved_rows",
    )(col_here, inverse, *crosses)


def rotated(offsets, value, row_count, col_count):
    per_child = col_count // CHILDREN
    ids = [(r, c) for r in range(row_count) for c in range(col_count)]

    def by(child, shift):
        if shift == 0:
            return lambda v: v
        pairs = [
            (r * col_count + c, ((r + shift) % row_count if c // per_child == child else r) * col_count + c)
            for r, c in ids
        ]
        return lambda v: lax.ppermute(v, ("row", "col"), pairs)

    for child in range(CHILDREN):
        value = lax.switch(offsets[child] % row_count, [by(child, k) for k in range(row_count)], value)
    return value


def gathered_cols(value, col_count):
    half = col_count // 2
    own = [value]
    for d in range(1, half):
        pairs = [(i, ((i // 2 + d) % half) * 2 + i % 2) for i in range(col_count)]
        own.append(lax.ppermute(value, "col", pairs))
    own = jnp.stack(own)
    return own, lax.ppermute(own, "col", [(i, i ^ 1) for i in range(col_count)])


def exchanged(parts, axis):
    return lax.all_to_all(parts, axis, split_axis=0, concat_axis=0, tiled=True)


def summed_rows(parts):
    own = jnp.sum(exchanged(parts, "row"), axis=0)
    return exchanged(jnp.broadcast_to(own[None], parts.shape), "row")


def shards(child_tiles, tile_dest, tile_counts, child_offsets):
    row_count = lax.axis_size("row")
    col_count = lax.axis_size("col")
    row_here = lax.axis_index("row")
    col_here = lax.axis_index("col")
    slot_count, size = child_tiles.shape[:2]
    tiles_col = NC // col_count // size
    width = PANELS * size
    slots = jnp.arange(slot_count, dtype=jnp.int32)
    cols = jnp.arange(col_count, dtype=jnp.int32)
    child_of = cols // (col_count // CHILDREN)
    offsets = jnp.sum(jnp.where(child_of[:, None] == jnp.arange(CHILDREN)[None, :], child_offsets[None, :], 0), axis=1)
    offset_here = jnp.sum(jnp.where(cols == col_here, offsets, 0))

    owner = jnp.where(slots < tile_counts[0, 0], tile_dest[:, 0] // tiles_col, -1)
    local_row = tile_dest[:, 1] + (offset_here + row_here) // row_count
    position = local_row * tiles_col + tile_dest[:, 0] % tiles_col
    earlier = (owner[:, None] == owner[None, :]) & (slots[None, :] < slots[:, None])
    bucket = jnp.where(owner >= 0, owner * CAPC + jnp.sum(earlier, axis=1), -1)
    hit = jnp.arange(col_count * CAPC, dtype=jnp.int32)[:, None] == bucket[None, :]
    picks = jnp.sum(jnp.where(hit, slots[None, :], 0), axis=1)
    places = jnp.sum(jnp.where(hit, position[None, :] + 1, 0), axis=1) - 1
    meta = jnp.concatenate([picks, places]).astype(jnp.int32)

    metas = exchanged(jnp.broadcast_to(meta, (row_count * col_count, meta.shape[0])), ("row", "col"))
    source = (row_here - offsets) % row_count
    chosen = (jnp.arange(row_count)[:, None] == source[None, :])[:, :, None]
    seen = jnp.sum(jnp.where(chosen, metas.reshape(row_count, col_count, -1), 0), axis=0)
    seen_picks, seen_places = seen[:, : col_count * CAPC], seen[:, col_count * CAPC :].reshape(col_count, col_count, CAPC)
    my_picks = jnp.sum(jnp.where(cols[:, None] == col_here, seen_picks, 0), axis=0)
    my_places = jnp.sum(jnp.where(cols[None, :, None] == col_here, seen_places, 0), axis=1).reshape(-1)
    half = col_count // 2
    order = jnp.stack([((col_here // 2 - d) % half) * 2 + (col_here + c) % 2 for c in range(2) for d in range(half)])
    ordered = order[:, None] == cols[None, :]
    lead_places = jnp.sum(jnp.where(ordered[:, :, None], seen_places[None, :, 0], 0), axis=1).reshape(-1)
    table = jnp.array(gram_table(col_count), jnp.int32).reshape(col_count, -1)
    spots = jnp.sum(jnp.where(ordered[:, :, None], table[None], 0), axis=1)
    col_scalar = col_here.reshape(1).astype(jnp.int32)

    lead = rotated(child_offsets, take_tiles(child_tiles, picks[:CAPC].astype(jnp.int32)), row_count, col_count)
    ready = lax.optimization_barrier((child_tiles, lead))[0]
    wide = size // CHUNKS
    tiles = [
        rotated(child_offsets, ready[:, :, c * wide : (c + 1) * wide], row_count, col_count) for c in range(CHUNKS)
    ]
    leads = [v.reshape(-1, size, size) for v in gathered_cols(lead, col_count)]
    gram_parts = gathered_cols(summed_rows(gram_slice(spots[0], lead_places, leads)), col_count)
    lead_high, lead_low = leading_split(lead_places, leads)
    crosses = []
    for tile in tiles:
        packed = take_tiles(tile, my_picks).reshape(col_count, CAPC, size, wide)
        arrived = exchanged(packed, "col").reshape(col_count * CAPC, size, wide)
        cross = cross_products(my_places, arrived, lead_high, lead_low)
        crosses.append(summed_rows(cross.reshape(row_count, width // row_count, -1)).reshape(width, -1))
    inverse = inverse_cholesky(spots.reshape(-1), gram_parts, width)
    return solved_rows(col_scalar, inverse, crosses)


def solution(mesh):
    return jax.shard_map(
        shards,
        mesh=mesh,
        in_specs=(P(("row", "col"), None, None), P(("row", "col"), None), P("row", "col"), P()),
        out_specs=P(None, "col"),
        check_vma=False,
    )
```

```python
import jax
import jax.numpy as jnp
from jax import lax
from jax.experimental import pallas as pl
from jax.experimental.pallas import tpu as pltpu
from jax.sharding import PartitionSpec as P

NC = 8192
PANELS = 4
CHILDREN = 4
CAPC = 2
RTD = 8
BLK = 128
GRAM_SLOTS = 5
CHUNKS = 2
FIRST = 3
HIGHEST = lax.Precision.HIGHEST
F32 = jnp.float32
BF16 = jnp.bfloat16
VMEM_LIMIT = 56 << 20


def split(x):
    high = x.astype(BF16)
    return high, (x - high.astype(F32)).astype(BF16)


def dot3(a_high, a_low, b_high, b_low):
    left = jnp.concatenate([a_high, a_high, a_low], axis=1)
    right = jnp.concatenate([b_high, b_low, b_high], axis=0)
    return jnp.dot(left, right, preferred_element_type=F32)


def params():
    return pltpu.CompilerParams(vmem_limit_bytes=VMEM_LIMIT)


def take_tiles(tiles, picks):
    count, (high, wide) = picks.shape[0], tiles.shape[1:]

    def kernel(pick_ref, in_ref, out_ref):
        out_ref[...] = in_ref[...]

    return pl.pallas_call(
        kernel,
        grid_spec=pltpu.PrefetchScalarGridSpec(
            num_scalar_prefetch=1,
            grid=(count,),
            in_specs=[pl.BlockSpec((1, high, wide), lambda i, pick: (pick[i], 0, 0))],
            out_specs=pl.BlockSpec((1, high, wide), lambda i, pick: (i, 0, 0)),
        ),
        out_shape=jax.ShapeDtypeStruct((count, high, wide), F32),
        cost_estimate=pl.CostEstimate(flops=0, bytes_accessed=8 * count * high * wide, transcendentals=0),
        name="take_tiles",
    )(picks, tiles)


def take_leads(tiles, picks, note):
    count, (high, wide), extra = picks.shape[0], tiles.shape[1:], note.shape[0]

    def kernel(pick_ref, in_ref, note_ref, out_ref):
        out_ref[0, :high] = in_ref[0]
        out_ref[0, high:] = note_ref[...]

    return pl.pallas_call(
        kernel,
        grid_spec=pltpu.PrefetchScalarGridSpec(
            num_scalar_prefetch=1,
            grid=(count,),
            in_specs=[
                pl.BlockSpec((1, high, wide), lambda i, pick: (pick[i], 0, 0)),
                pl.BlockSpec((extra, wide), lambda i, pick: (0, 0)),
            ],
            out_specs=pl.BlockSpec((1, high + extra, wide), lambda i, pick: (i, 0, 0)),
        ),
        out_shape=jax.ShapeDtypeStruct((count, high + extra, wide), F32),
        cost_estimate=pl.CostEstimate(flops=0, bytes_accessed=8 * count * high * wide, transcendentals=0),
        name="take_leads",
    )(picks, tiles, note)


def gram_table(col_count):
    blocks = col_count
    table = []
    for c in range(col_count):
        low = min(c, blocks - 1 - c)
        shared = [(i, j) for i in (low, blocks - 1 - low) for j in range(i, blocks)]
        mine = shared[::2] if c == low else shared[1::2]
        table.append((mine + mine[-1:])[: GRAM_SLOTS])
    return table


def place_leads(pos_ref, lead_refs, sum_ref, transposed):
    sum_ref[...] = jnp.zeros_like(sum_ref)
    count, size = lead_refs[0].shape[0], lead_refs[0].shape[2]
    for s, ref in enumerate(lead_refs):

        def place(r, _, s=s, ref=ref):
            pos = pos_ref[s * count + r]

            @pl.when(pos >= 0)
            def _():
                at_row = pl.ds(pl.multiple_of((pos // PANELS) * size, size), size)
                at_col = pl.ds(pl.multiple_of((pos % PANELS) * size, size), size)
                if transposed:
                    sum_ref[at_col, at_row] += ref[r, :size].T
                else:
                    sum_ref[at_row, at_col] += ref[r, :size]

            return 0

        lax.fori_loop(0, count, place, 0)


def gram_slice(mine, positions, leads):
    size = leads[0].shape[2]
    width, depth = PANELS * size, RTD * size

    def kernel(mine_ref, pos_ref, *refs):
        lead_refs, (out_ref, sum_ref, left_ref) = refs[: len(leads)], refs[len(leads) :]
        place_leads(pos_ref, lead_refs, sum_ref, False)

        def block(s, _):
            at_i = pl.ds(pl.multiple_of(mine_ref[2 * s] * BLK, BLK), BLK)
            at_j = pl.ds(pl.multiple_of(mine_ref[2 * s + 1] * BLK, BLK), BLK)
            at_s = pl.ds(pl.multiple_of(s * BLK, BLK), BLK)
            for k in range(RTD):
                rows = slice(k * size, (k + 1) * size)
                left_ref[:, rows] = sum_ref[rows, at_i].T
            a_high, a_low = split(left_ref[...])
            b_high, b_low = split(sum_ref[:, at_j])
            block_out = dot3(a_high, a_low, b_high, b_low)
            for g in range(BLK // 8):
                out_ref[g, :, at_s] = block_out[8 * g : 8 * g + 8]
            return 0

        lax.fori_loop(0, GRAM_SLOTS, block, 0)

    smem = pl.BlockSpec(memory_space=pltpu.SMEM)
    vmem = pl.BlockSpec(memory_space=pltpu.VMEM)
    return pl.pallas_call(
        kernel,
        in_specs=[smem, smem] + [vmem] * len(leads),
        out_specs=vmem,
        out_shape=jax.ShapeDtypeStruct((BLK // 8, 8, GRAM_SLOTS * BLK), F32),
        scratch_shapes=[pltpu.VMEM((depth, width), F32), pltpu.VMEM((BLK, depth), F32)],
        compiler_params=params(),
        cost_estimate=pl.CostEstimate(
            flops=6 * BLK * width * depth, bytes_accessed=4 * 16 * size * size, transcendentals=0
        ),
        name="gram_slice",
    )(mine, positions, *leads)


def leading_split(positions, leads):
    size = leads[0].shape[2]
    width, depth = PANELS * size, RTD * size

    def kernel(pos_ref, *refs):
        lead_refs, (high_ref, low_ref, sum_ref) = refs[: len(leads)], refs[len(leads) :]
        place_leads(pos_ref, lead_refs, sum_ref, True)

        def step(k, _):
            rows = pl.ds(pl.multiple_of(k * BLK, BLK), BLK)
            high_ref[rows, :], low_ref[rows, :] = split(sum_ref[rows, :])
            return 0

        lax.fori_loop(0, width // BLK, step, 0)

    smem = pl.BlockSpec(memory_space=pltpu.SMEM)
    vmem = pl.BlockSpec(memory_space=pltpu.VMEM)
    return pl.pallas_call(
        kernel,
        in_specs=[smem] + [vmem] * len(leads),
        out_specs=[vmem, vmem],
        out_shape=[jax.ShapeDtypeStruct((width, depth), BF16)] * 2,
        scratch_shapes=[pltpu.VMEM((width, depth), F32)],
        compiler_params=params(),
        cost_estimate=pl.CostEstimate(flops=0, bytes_accessed=12 << 20, transcendentals=0),
        name="leading_split",
    )(positions, *leads)


def cross_products(positions, tiles, lead_high, lead_low):
    size, wide = tiles.shape[1:]
    width, depth = lead_high.shape
    cols = PANELS * wide

    def kernel(pos_ref, tile_ref, high_ref, low_ref, out_ref):
        i = pl.program_id(0)

        @pl.when(i == 0)
        def _():
            out_ref[...] = jnp.zeros_like(out_ref)

        pos = pos_ref[i]

        @pl.when(pos >= 0)
        def _():
            at_row = pl.ds(pl.multiple_of((pos // PANELS) * size, size), size)
            at_col = pl.ds(pl.multiple_of((pos % PANELS) * wide, wide), wide)
            b_high, b_low = split(tile_ref[0])
            out_ref[:, at_col] += dot3(high_ref[:, at_row], low_ref[:, at_row], b_high, b_low)

    count = tiles.shape[0]
    return pl.pallas_call(
        kernel,
        grid_spec=pltpu.PrefetchScalarGridSpec(
            num_scalar_prefetch=1,
            grid=(count,),
            in_specs=[
                pl.BlockSpec((1, size, wide), lambda i, pos: (i, 0, 0)),
                pl.BlockSpec((width, depth), lambda i, pos: (0, 0), pipeline_mode=pl.Buffered(1)),
                pl.BlockSpec((width, depth), lambda i, pos: (0, 0), pipeline_mode=pl.Buffered(1)),
            ],
            out_specs=pl.BlockSpec((width, cols), lambda i, pos: (0, 0)),
        ),
        out_shape=jax.ShapeDtypeStruct((width, cols), F32),
        compiler_params=params(),
        cost_estimate=pl.CostEstimate(
            flops=6 * count * width * size * wide, bytes_accessed=16 << 20, transcendentals=0
        ),
        name="cross_products",
    )(positions, tiles, lead_high, lead_low)


def block_factor(block):
    tiles = BLK // 8
    lane = lax.broadcasted_iota(jnp.int32, (8, BLK), 1)
    sub = lax.broadcasted_iota(jnp.int32, (8, BLK), 0)
    full = lambda v: jnp.broadcast_to(v, (8, BLK))
    x = [block[8 * t : 8 * t + 8, :] for t in range(tiles)]
    out = []
    for t in range(tiles):
        base = 8 * t
        panel = lane // 8 == t
        rows = [full(x[t][p : p + 1, :]) for p in range(8)]
        a = {(p, q): full(rows[p][:, base + q : base + q + 1]) for p in range(8) for q in range(p, 8)}
        rows = [jnp.where(panel, jnp.where(lane == base + p, 1.0, 0.0), rows[p]) for p in range(8)]
        columns = {u: [full(x[u][:, base + p : base + p + 1]) for p in range(8)] for u in range(t + 1, tiles)}
        for u in range(t + 1, tiles):
            x[u] = jnp.where(panel, 0.0, x[u])
        scales = []
        for p in range(8):
            inverse = 1.0 / a[p, p]
            scale = lax.rsqrt(a[p, p])
            scales.append(scale * (1.5 - 0.5 * a[p, p] * scale * scale))
            scaled = rows[p] * inverse
            ratio = [a[p, q] * inverse for q in range(p + 1, 8)]
            for q in range(p + 1, 8):
                for r in range(q, 8):
                    a[q, r] = a[q, r] - a[p, q] * ratio[r - p - 1]
                rows[q] = rows[q] - a[p, q] * scaled
            for u in range(t + 1, tiles):
                for q in range(p + 1, 8):
                    columns[u][q] = columns[u][q] - columns[u][p] * ratio[q - p - 1]
                x[u] = x[u] - columns[u][p] * scaled
        tile = rows[0] * scales[0]
        for p in range(1, 8):
            tile = jnp.where(sub == p, rows[p] * scales[p], tile)
        out.append(jnp.where(lane <= sub + base, tile, 0.0))
    return jnp.concatenate(out, axis=0)


def eliminate(first, last, work_ref, out_ref, row_ref):
    width = work_ref.shape[1]

    def outer(k, _):
        at = pl.multiple_of(k * BLK, BLK)
        here = pl.ds(at, BLK)
        inverse = block_factor(work_ref[here, here])
        row_ref[...] = jnp.dot(inverse, work_ref[here, :], precision=HIGHEST, preferred_element_type=F32)
        row_ref[:, here] = inverse
        row = row_ref[...]
        lane = lax.broadcasted_iota(jnp.int32, (BLK, width), 1)
        out_ref[pl.ds(pl.multiple_of(at - first * BLK, BLK), BLK), :] = jnp.where(lane < at + BLK, row, 0.0)

        def inner(i, _):
            below = pl.ds(pl.multiple_of(i * BLK, BLK), BLK)
            factor = row_ref[:, below].T
            work_ref[below, here] = jnp.zeros((BLK, BLK), F32)
            work_ref[below, :] -= jnp.dot(factor, row, precision=HIGHEST, preferred_element_type=F32)
            return 0

        lax.fori_loop(k + 1, width // BLK, inner, 0)
        return 0

    lax.fori_loop(first, last, outer, 0)


def inverse_cholesky_start(spots, parts, width):
    def kernel(spot_ref, *refs):
        part_refs, (out_ref, rest_ref, work_ref, row_ref) = refs[: len(parts)], refs[len(parts) :]
        for n, ref in enumerate(part_refs):
            count = ref.shape[0]

            def fill(s, _, n=n, ref=ref, count=count):
                q, r = s // GRAM_SLOTS, s % GRAM_SLOTS
                at = 2 * (n * count * GRAM_SLOTS + s)
                row = pl.multiple_of(spot_ref[at] * BLK, BLK)
                col = pl.multiple_of(spot_ref[at + 1] * BLK, BLK)
                lanes = pl.ds(pl.multiple_of(r * BLK, BLK), BLK)
                for g in range(BLK // 8):
                    work_ref[pl.ds(row + 8 * g, 8), pl.ds(col, BLK)] = ref[q, g, :, lanes]
                return 0

            lax.fori_loop(0, count * GRAM_SLOTS, fill, 0)
        eliminate(0, FIRST, work_ref, out_ref, row_ref)
        rest_ref[...] = work_ref[FIRST * BLK :, :]

    smem = pl.BlockSpec(memory_space=pltpu.SMEM)
    vmem = pl.BlockSpec(memory_space=pltpu.VMEM)
    return pl.pallas_call(
        kernel,
        in_specs=[smem] + [vmem] * len(parts),
        out_specs=[vmem, vmem],
        out_shape=[
            jax.ShapeDtypeStruct((FIRST * BLK, width), F32),
            jax.ShapeDtypeStruct((width - FIRST * BLK, width), F32),
        ],
        scratch_shapes=[pltpu.VMEM((width, width), F32), pltpu.VMEM((BLK, width), F32)],
        compiler_params=params(),
        cost_estimate=pl.CostEstimate(flops=30 << 30, bytes_accessed=8 << 20, transcendentals=0),
        name="inverse_cholesky_start",
    )(spots, *parts)


def inverse_cholesky_end(rest):
    low, width = rest.shape
    first = (width - low) // BLK

    def kernel(rest_ref, out_ref, work_ref, row_ref):
        work_ref[first * BLK :, :] = rest_ref[...]
        eliminate(first, width // BLK, work_ref, out_ref, row_ref)

    vmem = pl.BlockSpec(memory_space=pltpu.VMEM)
    return pl.pallas_call(
        kernel,
        in_specs=[vmem],
        out_specs=vmem,
        out_shape=jax.ShapeDtypeStruct((low, width), F32),
        scratch_shapes=[pltpu.VMEM((width, width), F32), pltpu.VMEM((BLK, width), F32)],
        compiler_params=params(),
        cost_estimate=pl.CostEstimate(flops=30 << 30, bytes_accessed=8 << 20, transcendentals=0),
        name="inverse_cholesky_end",
    )(rest)


def solved_rows(col_here, inverses, crosses):
    width, cols = crosses[0].shape[0], sum(c.shape[1] for c in crosses)
    wide = crosses[0].shape[1] // PANELS
    size = wide * len(crosses)

    def kernel(col_ref, *refs):
        inv_refs, refs = refs[: len(inverses)], refs[len(inverses) :]
        cross_refs, (out_ref, high_ref, low_ref) = refs[: len(crosses)], refs[len(crosses) :]
        i = pl.program_id(0)

        @pl.when(i == 0)
        def _():
            at = 0
            for ref in inv_refs:
                rows = slice(at, at + ref.shape[0])
                high_ref[rows, :], low_ref[rows, :] = split(ref[...])
                at += ref.shape[0]

        b_high, b_low = split(jnp.concatenate([ref[...] for ref in cross_refs], axis=1))
        first = col_ref[0] * cols + i * size
        step = 256
        for k in range(width // step):
            rows, done = slice(k * step, (k + 1) * step), (k + 1) * step
            value = dot3(high_ref[rows, :done], low_ref[rows, :done], b_high[:done], b_low[:done])
            row = lax.broadcasted_iota(jnp.int32, (step, size), 0) + k * step
            col = lax.broadcasted_iota(jnp.int32, (step, size), 1) + first
            out_ref[rows, :] = jnp.where(col >= row, value, 0.0)

    return pl.pallas_call(
        kernel,
        grid_spec=pltpu.PrefetchScalarGridSpec(
            num_scalar_prefetch=1,
            grid=(cols // size,),
            in_specs=[
                pl.BlockSpec(part.shape, lambda i, col: (0, 0), pipeline_mode=pl.Buffered(1)) for part in inverses
            ]
            + [pl.BlockSpec((width, wide), lambda i, col: (0, i))] * len(crosses),
            out_specs=pl.BlockSpec((width, size), lambda i, col: (0, i)),
            scratch_shapes=[pltpu.VMEM((width, width), BF16)] * 2,
        ),
        out_shape=jax.ShapeDtypeStruct((width, cols), F32),
        compiler_params=params(),
        cost_estimate=pl.CostEstimate(flops=6 * width * width * cols, bytes_accessed=12 << 20, transcendentals=0),
        name="solved_rows",
    )(col_here, *inverses, *crosses)


def rotated(amount, value, row_count):
    def by(shift):
        if shift == 0:
            return lambda v: v
        pairs = [(i, (i + shift) % row_count) for i in range(row_count)]
        return lambda v: lax.ppermute(v, "row", pairs)

    return lax.switch(amount, [by(k) for k in range(row_count)], value)


def pair_steps(value, col_count):
    half = col_count // 2
    steps = [[(i, ((i // 2 + d) % half) * 2 + i % 2) for i in range(col_count)] for d in range(1, half)]
    return [value] + [lax.ppermute(value, "col", pairs) for pairs in steps]


def both_cores(own, col_count):
    own = jnp.stack(own)
    return own, lax.ppermute(own, "col", [(i, i ^ 1) for i in range(col_count)])


def exchanged(parts, axis):
    return lax.all_to_all(parts, axis, split_axis=0, concat_axis=0, tiled=True)


def summed_rows(parts):
    own = jnp.sum(exchanged(parts, "row"), axis=0)
    return exchanged(jnp.broadcast_to(own[None], parts.shape), "row")


def shards(child_tiles, tile_dest, tile_counts, child_offsets):
    row_count = lax.axis_size("row")
    col_count = lax.axis_size("col")
    row_here = lax.axis_index("row")
    col_here = lax.axis_index("col")
    slot_count, size = child_tiles.shape[:2]
    tiles_col = NC // col_count // size
    width = PANELS * size
    slots = jnp.arange(slot_count, dtype=jnp.int32)
    cols = jnp.arange(col_count, dtype=jnp.int32)
    child_of = cols // (col_count // CHILDREN)
    offsets = jnp.sum(jnp.where(child_of[:, None] == jnp.arange(CHILDREN)[None, :], child_offsets[None, :], 0), axis=1)
    offset_here = jnp.sum(jnp.where(cols == col_here, offsets, 0))
    amount = offset_here % row_count

    owner = jnp.where(slots < tile_counts[0, 0], tile_dest[:, 0] // tiles_col, -1)
    local_row = tile_dest[:, 1] + (offset_here + row_here) // row_count
    position = local_row * tiles_col + tile_dest[:, 0] % tiles_col
    earlier = (owner[:, None] == owner[None, :]) & (slots[None, :] < slots[:, None])
    bucket = jnp.where(owner >= 0, owner * CAPC + jnp.sum(earlier, axis=1), -1)
    hit = jnp.arange(col_count * CAPC, dtype=jnp.int32)[:, None] == bucket[None, :]
    picks = jnp.sum(jnp.where(hit, slots[None, :], 0), axis=1)
    places = jnp.sum(jnp.where(hit, position[None, :] + 1, 0), axis=1) - 1
    meta = jnp.concatenate([picks, places]).astype(jnp.int32)

    wide = size // CHUNKS
    note = jnp.broadcast_to(jnp.pad(meta.astype(F32), (0, size - meta.shape[0])), (8, size))
    lead = rotated(amount, take_leads(child_tiles, picks[:CAPC].astype(jnp.int32), note), row_count)
    near = pair_steps(lead, col_count)
    ready = lax.optimization_barrier((child_tiles, lead))[0]
    tiles = [rotated(amount, ready[:, :, c * wide : (c + 1) * wide], row_count) for c in range(CHUNKS)]
    near, tiles = lax.optimization_barrier((near, tiles))

    stacks = both_cores(near, col_count)
    notes = jnp.concatenate([v[:, 0, size, : meta.shape[0]] for v in stacks]).astype(jnp.int32)
    my_picks = notes[0, : col_count * CAPC]
    places = notes[:, col_count * CAPC :].reshape(col_count, col_count, CAPC)
    lead_places = places[:, 0].reshape(-1)
    half = col_count // 2
    order = jnp.stack([((col_here // 2 - d) % half) * 2 + (col_here + c) % 2 for c in range(2) for d in range(half)])
    ordered = order[:, None] == cols[None, :]
    mine = jnp.sum(jnp.where(cols[None, :, None] == col_here, places, 0), axis=1)
    my_places = jnp.sum(jnp.where(ordered[:, :, None], mine[:, None, :], 0), axis=0).reshape(-1)
    table = jnp.array(gram_table(col_count), jnp.int32).reshape(col_count, -1)
    spots = jnp.sum(jnp.where(ordered[:, :, None], table[None], 0), axis=1)
    col_scalar = col_here.reshape(1).astype(jnp.int32)

    leads = [v.reshape(-1, *v.shape[2:]) for v in stacks]
    gram_part = summed_rows(gram_slice(spots[0], lead_places, leads))
    gram_parts = both_cores(pair_steps(gram_part, col_count), col_count)
    lead_high, lead_low = leading_split(lead_places, leads)
    crosses = []
    for tile in tiles:
        packed = take_tiles(tile, my_picks).reshape(col_count, CAPC, size, wide)
        arrived = exchanged(packed, "col").reshape(col_count * CAPC, size, wide)
        cross = cross_products(my_places, arrived, lead_high, lead_low)
        crosses.append(summed_rows(cross.reshape(row_count, width // row_count, -1)).reshape(width, -1))
    begun, rest = inverse_cholesky_start(spots.reshape(-1), gram_parts, width)
    ended = inverse_cholesky_end(rest)
    return solved_rows(col_scalar, [begun, ended], crosses)


def solution(mesh):
    return jax.shard_map(
        shards,
        mesh=mesh,
        in_specs=(P(("row", "col"), None, None), P(("row", "col"), None), P("row", "col"), P()),
        out_specs=P(None, "col"),
        check_vma=False,
    )
```

```python
import jax
import jax.numpy as jnp
from jax import lax
from jax.experimental import pallas as pl
from jax.experimental.pallas import tpu as pltpu
from jax.sharding import PartitionSpec as P

NC = 8192
PANELS = 4
CHILDREN = 4
CAPC = 2
RTD = 8
BLK = 128
GRAM_SLOTS = 5
FIRST = 3
CHUNKS = 2
CHOL_COST = 200 << 30
HIGHEST = lax.Precision.HIGHEST
F32 = jnp.float32
BF16 = jnp.bfloat16
VMEM_LIMIT = 56 << 20


def split(x):
    high = x.astype(BF16)
    return high, (x - high.astype(F32)).astype(BF16)


def dot3(a_high, a_low, b_high, b_low):
    left = jnp.concatenate([a_high, a_high, a_low], axis=1)
    right = jnp.concatenate([b_high, b_low, b_high], axis=0)
    return jnp.dot(left, right, preferred_element_type=F32)


def params():
    return pltpu.CompilerParams(vmem_limit_bytes=VMEM_LIMIT)


def take_tiles(tiles, picks):
    count, (high, wide) = picks.shape[0], tiles.shape[1:]

    def kernel(pick_ref, in_ref, out_ref):
        out_ref[...] = in_ref[...]

    return pl.pallas_call(
        kernel,
        grid_spec=pltpu.PrefetchScalarGridSpec(
            num_scalar_prefetch=1,
            grid=(count,),
            in_specs=[pl.BlockSpec((1, high, wide), lambda i, pick: (pick[i], 0, 0))],
            out_specs=pl.BlockSpec((1, high, wide), lambda i, pick: (i, 0, 0)),
        ),
        out_shape=jax.ShapeDtypeStruct((count, high, wide), F32),
        cost_estimate=pl.CostEstimate(flops=0, bytes_accessed=8 * count * high * wide, transcendentals=0),
        name="take_tiles",
    )(picks, tiles)


def take_leads(tiles, picks, note):
    count, (high, wide), extra = picks.shape[0], tiles.shape[1:], note.shape[0]

    def kernel(pick_ref, in_ref, note_ref, out_ref):
        out_ref[0, :high] = in_ref[0]
        out_ref[0, high:] = note_ref[...]

    return pl.pallas_call(
        kernel,
        grid_spec=pltpu.PrefetchScalarGridSpec(
            num_scalar_prefetch=1,
            grid=(count,),
            in_specs=[
                pl.BlockSpec((1, high, wide), lambda i, pick: (pick[i], 0, 0)),
                pl.BlockSpec((extra, wide), lambda i, pick: (0, 0)),
            ],
            out_specs=pl.BlockSpec((1, high + extra, wide), lambda i, pick: (i, 0, 0)),
        ),
        out_shape=jax.ShapeDtypeStruct((count, high + extra, wide), F32),
        cost_estimate=pl.CostEstimate(flops=0, bytes_accessed=8 * count * high * wide, transcendentals=0),
        name="take_leads",
    )(picks, tiles, note)


def gram_table(col_count):
    blocks = col_count
    table = []
    for c in range(col_count):
        low = min(c, blocks - 1 - c)
        shared = [(i, j) for i in (low, blocks - 1 - low) for j in range(i, blocks)]
        mine = shared[::2] if c == low else shared[1::2]
        table.append((mine + mine[-1:])[: GRAM_SLOTS])
    return table


def place_leads(pos_ref, lead_refs, sum_ref, transposed):
    sum_ref[...] = jnp.zeros_like(sum_ref)
    count, size = lead_refs[0].shape[0], lead_refs[0].shape[2]
    for s, ref in enumerate(lead_refs):

        def place(r, _, s=s, ref=ref):
            pos = pos_ref[s * count + r]

            @pl.when(pos >= 0)
            def _():
                at_row = pl.ds(pl.multiple_of((pos // PANELS) * size, size), size)
                at_col = pl.ds(pl.multiple_of((pos % PANELS) * size, size), size)
                if transposed:
                    sum_ref[at_col, at_row] += ref[r, :size].T
                else:
                    sum_ref[at_row, at_col] += ref[r, :size]

            return 0

        lax.fori_loop(0, count, place, 0)


def gram_slice(mine, positions, leads):
    size = leads[0].shape[2]
    width, depth = PANELS * size, RTD * size

    def kernel(mine_ref, pos_ref, *refs):
        lead_refs, (out_ref, sum_ref, left_ref) = refs[: len(leads)], refs[len(leads) :]
        place_leads(pos_ref, lead_refs, sum_ref, False)

        def block(s, _):
            at_i = pl.ds(pl.multiple_of(mine_ref[2 * s] * BLK, BLK), BLK)
            at_j = pl.ds(pl.multiple_of(mine_ref[2 * s + 1] * BLK, BLK), BLK)
            at_s = pl.ds(pl.multiple_of(s * BLK, BLK), BLK)
            for k in range(RTD):
                rows = slice(k * size, (k + 1) * size)
                left_ref[:, rows] = sum_ref[rows, at_i].T
            a_high, a_low = split(left_ref[...])
            b_high, b_low = split(sum_ref[:, at_j])
            block_out = dot3(a_high, a_low, b_high, b_low)
            for g in range(BLK // 8):
                out_ref[g, :, at_s] = block_out[8 * g : 8 * g + 8]
            return 0

        lax.fori_loop(0, GRAM_SLOTS, block, 0)

    smem = pl.BlockSpec(memory_space=pltpu.SMEM)
    vmem = pl.BlockSpec(memory_space=pltpu.VMEM)
    return pl.pallas_call(
        kernel,
        in_specs=[smem, smem] + [vmem] * len(leads),
        out_specs=vmem,
        out_shape=jax.ShapeDtypeStruct((BLK // 8, 8, GRAM_SLOTS * BLK), F32),
        scratch_shapes=[pltpu.VMEM((depth, width), F32), pltpu.VMEM((BLK, depth), F32)],
        compiler_params=params(),
        cost_estimate=pl.CostEstimate(
            flops=6 * BLK * width * depth, bytes_accessed=4 * 16 * size * size, transcendentals=0
        ),
        name="gram_slice",
    )(mine, positions, *leads)


def leading_split(positions, leads):
    size = leads[0].shape[2]
    width, depth = PANELS * size, RTD * size

    def kernel(pos_ref, *refs):
        lead_refs, (high_ref, low_ref, sum_ref) = refs[: len(leads)], refs[len(leads) :]
        place_leads(pos_ref, lead_refs, sum_ref, True)

        def step(k, _):
            rows = pl.ds(pl.multiple_of(k * BLK, BLK), BLK)
            high_ref[rows, :], low_ref[rows, :] = split(sum_ref[rows, :])
            return 0

        lax.fori_loop(0, width // BLK, step, 0)

    smem = pl.BlockSpec(memory_space=pltpu.SMEM)
    vmem = pl.BlockSpec(memory_space=pltpu.VMEM)
    return pl.pallas_call(
        kernel,
        in_specs=[smem] + [vmem] * len(leads),
        out_specs=[vmem, vmem],
        out_shape=[jax.ShapeDtypeStruct((width, depth), BF16)] * 2,
        scratch_shapes=[pltpu.VMEM((width, depth), F32)],
        compiler_params=params(),
        cost_estimate=pl.CostEstimate(flops=0, bytes_accessed=12 << 20, transcendentals=0),
        name="leading_split",
    )(positions, *leads)


def cross_products(positions, groups, lead_high, lead_low):
    width, depth = lead_high.shape
    size = groups[0][0][0].shape[-2]
    chunks = len(groups[0][0])
    count = sum(n for _, n in groups) * CAPC
    step = 256

    def kernel(pos_ref, *refs):
        tile_refs, (high_ref, low_ref, out_ref) = refs[: len(groups) * chunks], refs[len(groups) * chunks :]
        out_ref[...] = jnp.zeros_like(out_ref)
        first = 0
        for g, (_, n) in enumerate(groups):
            parts = tile_refs[g * chunks : (g + 1) * chunks]

            def place(i, _, parts=parts, first=first):
                pos = pos_ref[first + i]

                @pl.when(pos >= 0)
                def _():
                    at_row = pl.ds(pl.multiple_of((pos // PANELS) * size, size), size)
                    at_col = pl.ds(pl.multiple_of((pos % PANELS) * size, size), size)
                    b_high, b_low = split(jnp.concatenate([ref[i // CAPC, i % CAPC] for ref in parts], axis=1))
                    dot = lambda x, y: jnp.dot(x, y, preferred_element_type=F32)
                    for m in range(0, width, step):
                        a_high, a_low = high_ref[m : m + step, at_row], low_ref[m : m + step, at_row]
                        out_ref[m : m + step, at_col] += dot(a_high, b_high) + dot(a_high, b_low) + dot(a_low, b_high)

                return 0

            lax.fori_loop(0, n * CAPC, place, 0)
            first += n * CAPC

    return pl.pallas_call(
        kernel,
        grid_spec=pltpu.PrefetchScalarGridSpec(
            num_scalar_prefetch=1,
            grid=(1,),
            in_specs=[
                pl.BlockSpec((n, *v.shape[1:]), lambda i, pos: (0, 0, 0, 0), pipeline_mode=pl.Buffered(1))
                for vs, n in groups
                for v in vs
            ]
            + [pl.BlockSpec((width, depth), lambda i, pos: (0, 0), pipeline_mode=pl.Buffered(1))] * 2,
            out_specs=pl.BlockSpec((width, PANELS * size), lambda i, pos: (0, 0), pipeline_mode=pl.Buffered(1)),
        ),
        out_shape=jax.ShapeDtypeStruct((width, PANELS * size), F32),
        compiler_params=params(),
        cost_estimate=pl.CostEstimate(
            flops=6 * count * width * size * size, bytes_accessed=16 << 20, transcendentals=0
        ),
        name="cross_products",
    )(positions, *[v for vs, _ in groups for v in vs], lead_high, lead_low)


def block_factor(block):
    tiles = BLK // 8
    lane = lax.broadcasted_iota(jnp.int32, (8, BLK), 1)
    sub = lax.broadcasted_iota(jnp.int32, (8, BLK), 0)
    full = lambda v: jnp.broadcast_to(v, (8, BLK))
    x = [block[8 * t : 8 * t + 8, :] for t in range(tiles)]
    out = []
    for t in range(tiles):
        base = 8 * t
        panel = lane // 8 == t
        rows = [full(x[t][p : p + 1, :]) for p in range(8)]
        a = {(p, q): full(rows[p][:, base + q : base + q + 1]) for p in range(8) for q in range(p, 8)}
        rows = [jnp.where(panel, jnp.where(lane == base + p, 1.0, 0.0), rows[p]) for p in range(8)]
        columns = {u: [full(x[u][:, base + p : base + p + 1]) for p in range(8)] for u in range(t + 1, tiles)}
        for u in range(t + 1, tiles):
            x[u] = jnp.where(panel, 0.0, x[u])
        scales = []
        for p in range(8):
            inverse = 1.0 / a[p, p]
            scale = lax.rsqrt(a[p, p])
            scales.append(scale * (1.5 - 0.5 * a[p, p] * scale * scale))
            scaled = rows[p] * inverse
            ratio = [a[p, q] * inverse for q in range(p + 1, 8)]
            for q in range(p + 1, 8):
                for r in range(q, 8):
                    a[q, r] = a[q, r] - a[p, q] * ratio[r - p - 1]
                rows[q] = rows[q] - a[p, q] * scaled
            for u in range(t + 1, tiles):
                for q in range(p + 1, 8):
                    columns[u][q] = columns[u][q] - columns[u][p] * ratio[q - p - 1]
                x[u] = x[u] - columns[u][p] * scaled
        tile = rows[0] * scales[0]
        for p in range(1, 8):
            tile = jnp.where(sub == p, rows[p] * scales[p], tile)
        out.append(jnp.where(lane <= sub + base, tile, 0.0))
    return jnp.concatenate(out, axis=0)


def eliminate(first, last, work_ref, out_ref, row_ref):
    width = work_ref.shape[1]

    def outer(k, _):
        at = pl.multiple_of(k * BLK, BLK)
        here = pl.ds(at, BLK)
        inverse = block_factor(work_ref[here, here])
        row_ref[...] = jnp.dot(inverse, work_ref[here, :], precision=HIGHEST, preferred_element_type=F32)
        row_ref[:, here] = inverse
        row = row_ref[...]
        lane = lax.broadcasted_iota(jnp.int32, (BLK, width), 1)
        out_ref[pl.ds(pl.multiple_of(at - first * BLK, BLK), BLK), :] = jnp.where(lane < at + BLK, row, 0.0)

        def inner(i, _):
            below = pl.ds(pl.multiple_of(i * BLK, BLK), BLK)
            factor = row_ref[:, below].T
            work_ref[below, here] = jnp.zeros((BLK, BLK), F32)
            work_ref[below, :] -= jnp.dot(factor, row, precision=HIGHEST, preferred_element_type=F32)
            return 0

        lax.fori_loop(k + 1, width // BLK, inner, 0)
        return 0

    lax.fori_loop(first, last, outer, 0)


def inverse_cholesky_start(spots, parts, width):
    def kernel(spot_ref, *refs):
        part_refs, (out_ref, rest_ref, work_ref, row_ref) = refs[: len(parts)], refs[len(parts) :]
        for n, ref in enumerate(part_refs):
            count = ref.shape[0]

            def fill(s, _, n=n, ref=ref, count=count):
                q, r = s // GRAM_SLOTS, s % GRAM_SLOTS
                at = 2 * (n * count * GRAM_SLOTS + s)
                row = pl.multiple_of(spot_ref[at] * BLK, BLK)
                col = pl.multiple_of(spot_ref[at + 1] * BLK, BLK)
                lanes = pl.ds(pl.multiple_of(r * BLK, BLK), BLK)
                for g in range(BLK // 8):
                    work_ref[pl.ds(row + 8 * g, 8), pl.ds(col, BLK)] = ref[q, g, :, lanes]
                return 0

            lax.fori_loop(0, count * GRAM_SLOTS, fill, 0)
        eliminate(0, FIRST, work_ref, out_ref, row_ref)
        rest_ref[...] = work_ref[FIRST * BLK :, :]

    smem = pl.BlockSpec(memory_space=pltpu.SMEM)
    vmem = pl.BlockSpec(memory_space=pltpu.VMEM)
    return pl.pallas_call(
        kernel,
        in_specs=[smem] + [vmem] * len(parts),
        out_specs=[vmem, vmem],
        out_shape=[
            jax.ShapeDtypeStruct((FIRST * BLK, width), F32),
            jax.ShapeDtypeStruct((width - FIRST * BLK, width), F32),
        ],
        scratch_shapes=[pltpu.VMEM((width, width), F32), pltpu.VMEM((BLK, width), F32)],
        compiler_params=params(),
        cost_estimate=pl.CostEstimate(flops=CHOL_COST, bytes_accessed=8 << 20, transcendentals=0),
        name="inverse_cholesky_start",
    )(spots, *parts)


def inverse_cholesky_end(rest):
    low, width = rest.shape
    first = (width - low) // BLK

    def kernel(rest_ref, out_ref, work_ref, row_ref):
        work_ref[first * BLK :, :] = rest_ref[...]
        eliminate(first, width // BLK, work_ref, out_ref, row_ref)

    vmem = pl.BlockSpec(memory_space=pltpu.VMEM)
    return pl.pallas_call(
        kernel,
        in_specs=[vmem],
        out_specs=vmem,
        out_shape=jax.ShapeDtypeStruct((low, width), F32),
        scratch_shapes=[pltpu.VMEM((width, width), F32), pltpu.VMEM((BLK, width), F32)],
        compiler_params=params(),
        cost_estimate=pl.CostEstimate(flops=CHOL_COST, bytes_accessed=8 << 20, transcendentals=0),
        name="inverse_cholesky_end",
    )(rest)


def solved_rows(col_here, inverses, crosses):
    width, cols = crosses[0].shape[0], sum(c.shape[1] for c in crosses)
    wide = crosses[0].shape[1] // PANELS
    size = wide * len(crosses)

    def kernel(col_ref, *refs):
        inv_refs, refs = refs[: len(inverses)], refs[len(inverses) :]
        cross_refs, (out_ref, high_ref, low_ref) = refs[: len(crosses)], refs[len(crosses) :]
        i = pl.program_id(0)

        @pl.when(i == 0)
        def _():
            at = 0
            for ref in inv_refs:
                rows = slice(at, at + ref.shape[0])
                high_ref[rows, :], low_ref[rows, :] = split(ref[...])
                at += ref.shape[0]

        b_high, b_low = split(jnp.concatenate([ref[...] for ref in cross_refs], axis=1))
        first = col_ref[0] * cols + i * size
        step = 256
        for k in range(width // step):
            rows, done = slice(k * step, (k + 1) * step), (k + 1) * step
            value = dot3(high_ref[rows, :done], low_ref[rows, :done], b_high[:done], b_low[:done])
            row = lax.broadcasted_iota(jnp.int32, (step, size), 0) + k * step
            col = lax.broadcasted_iota(jnp.int32, (step, size), 1) + first
            out_ref[rows, :] = jnp.where(col >= row, value, 0.0)

    return pl.pallas_call(
        kernel,
        grid_spec=pltpu.PrefetchScalarGridSpec(
            num_scalar_prefetch=1,
            grid=(cols // size,),
            in_specs=[
                pl.BlockSpec(part.shape, lambda i, col: (0, 0), pipeline_mode=pl.Buffered(1)) for part in inverses
            ]
            + [pl.BlockSpec((width, wide), lambda i, col: (0, i))] * len(crosses),
            out_specs=pl.BlockSpec((width, size), lambda i, col: (0, i)),
            scratch_shapes=[pltpu.VMEM((width, width), BF16)] * 2,
        ),
        out_shape=jax.ShapeDtypeStruct((width, cols), F32),
        compiler_params=params(),
        cost_estimate=pl.CostEstimate(flops=6 * width * width * cols, bytes_accessed=12 << 20, transcendentals=0),
        name="solved_rows",
    )(col_here, *inverses, *crosses)


def rotated(amount, value, row_count):
    def by(shift):
        if shift == 0:
            return lambda v: v
        pairs = [(i, (i + shift) % row_count) for i in range(row_count)]
        return lambda v: lax.ppermute(v, "row", pairs)

    return lax.switch(amount, [by(k) for k in range(row_count)], value)


def step_pairs(step, col_count):
    half = col_count // 2
    return [(i, ((i // 2 + step) % half) * 2 + i % 2) for i in range(col_count)]


def pair_steps(value, col_count):
    return [value] + [lax.ppermute(value, "col", step_pairs(d, col_count)) for d in range(1, col_count // 2)]


def both_cores(own, col_count):
    own = jnp.stack(own)
    return own, lax.ppermute(own, "col", [(i, i ^ 1) for i in range(col_count)])


def exchanged(parts, axis):
    return lax.all_to_all(parts, axis, split_axis=0, concat_axis=0, tiled=True)


def summed_rows(parts):
    own = jnp.sum(exchanged(parts, "row"), axis=0)
    return exchanged(jnp.broadcast_to(own[None], parts.shape), "row")


def shards(child_tiles, tile_dest, tile_counts, child_offsets):
    row_count = lax.axis_size("row")
    col_count = lax.axis_size("col")
    row_here = lax.axis_index("row")
    col_here = lax.axis_index("col")
    slot_count, size = child_tiles.shape[:2]
    tiles_col = NC // col_count // size
    width = PANELS * size
    slots = jnp.arange(slot_count, dtype=jnp.int32)
    cols = jnp.arange(col_count, dtype=jnp.int32)
    child_of = cols // (col_count // CHILDREN)
    offsets = jnp.sum(jnp.where(child_of[:, None] == jnp.arange(CHILDREN)[None, :], child_offsets[None, :], 0), axis=1)
    offset_here = jnp.sum(jnp.where(cols == col_here, offsets, 0))
    amount = offset_here % row_count

    owner = jnp.where(slots < tile_counts[0, 0], tile_dest[:, 0] // tiles_col, -1)
    local_row = tile_dest[:, 1] + (offset_here + row_here) // row_count
    position = local_row * tiles_col + tile_dest[:, 0] % tiles_col
    earlier = (owner[:, None] == owner[None, :]) & (slots[None, :] < slots[:, None])
    bucket = jnp.where(owner >= 0, owner * CAPC + jnp.sum(earlier, axis=1), -1)
    hit = jnp.arange(col_count * CAPC, dtype=jnp.int32)[:, None] == bucket[None, :]
    picks = jnp.sum(jnp.where(hit, slots[None, :], 0), axis=1)
    places = jnp.sum(jnp.where(hit, position[None, :] + 1, 0), axis=1) - 1
    meta = jnp.concatenate([picks, places]).astype(jnp.int32)

    note = jnp.broadcast_to(jnp.pad(meta.astype(F32), (0, size - meta.shape[0])), (8, size))
    lead = rotated(amount, take_leads(child_tiles, picks[:CAPC].astype(jnp.int32), note), row_count)
    near = pair_steps(lead, col_count)
    my_picks = lead[0, size, : col_count * CAPC].astype(jnp.int32).reshape(col_count, CAPC)
    half = col_count // 2
    steps = jnp.arange(half)[:, None]
    targets = ((col_here // 2 + steps) % half) * 2 + (col_here + jnp.arange(2)[None, :]) % 2
    chosen = targets[:, :, None] == cols
    my_picks = jnp.sum(jnp.where(chosen[..., None], my_picks, 0), axis=2).reshape(half, 2 * CAPC)
    wide = size // CHUNKS
    far, others, stacks = [], [], None
    for c in range(CHUNKS):
        ready = child_tiles[:, :, c * wide : (c + 1) * wide]
        if c == 0:
            ready, _, my_picks = lax.optimization_barrier((ready, lead, my_picks))
        else:
            ready, _, _ = lax.optimization_barrier((ready, packed, stacks[0]))
        tiles = rotated(amount, ready, row_count)
        if c == 0:
            near, tiles = lax.optimization_barrier((near, tiles))
            stacks = both_cores(near, col_count)
        else:
            far, tiles = lax.optimization_barrier((far, tiles))
        packed = [take_tiles(tiles, my_picks[d]).reshape(2, CAPC, size, wide) for d in range(half)]
        if c == CHUNKS - 1:
            stacks, packed = lax.optimization_barrier((stacks, packed))
        far.append([packed[0]] + [lax.ppermute(packed[d], "col", step_pairs(d, col_count)) for d in range(1, half)])

    notes = jnp.concatenate([v[:, 0, size, : meta.shape[0]] for v in stacks]).astype(jnp.int32)
    places = notes[:, col_count * CAPC :].reshape(col_count, col_count, CAPC)
    lead_places = places[:, 0].reshape(-1)
    order = jnp.stack([((col_here // 2 - d) % half) * 2 + (col_here + c) % 2 for c in range(2) for d in range(half)])
    ordered = order[:, None] == cols[None, :]
    my_places = jnp.sum(jnp.where(cols[None, :, None] == col_here, places, 0), axis=1).reshape(-1)
    table = jnp.array(gram_table(col_count), jnp.int32).reshape(col_count, -1)
    spots = jnp.sum(jnp.where(ordered[:, :, None], table[None], 0), axis=1)
    col_scalar = col_here.reshape(1).astype(jnp.int32)

    leads = [v.reshape(-1, *v.shape[2:]) for v in stacks]
    gram_part = summed_rows(gram_slice(spots[0], lead_places, leads))
    far, gram_part = lax.optimization_barrier((far, gram_part))
    swap = [(i, i ^ 1) for i in range(col_count)]
    others = [lax.ppermute(jnp.stack([v[1] for v in chunk]), "col", swap) for chunk in far]
    gram_parts = both_cores(pair_steps(gram_part, col_count), col_count)
    lead_high, lead_low = leading_split(lead_places, leads)
    cross = cross_products(my_places, [(v, 1) for v in zip(*far)] + [(others, half)], lead_high, lead_low)
    cross = summed_rows(cross.reshape(row_count, width // row_count, -1)).reshape(width, -1)
    begun, rest = inverse_cholesky_start(spots.reshape(-1), gram_parts, width)
    ended = inverse_cholesky_end(rest)
    return solved_rows(col_scalar, [begun, ended], [cross])


def solution(mesh):
    return jax.shard_map(
        shards,
        mesh=mesh,
        in_specs=(P(("row", "col"), None, None), P(("row", "col"), None), P("row", "col"), P()),
        out_specs=P(None, "col"),
        check_vma=False,
    )
```

```python
import jax
import jax.numpy as jnp
from jax import lax
from jax.experimental import pallas as pl
from jax.experimental.pallas import tpu as pltpu
from jax.sharding import PartitionSpec as P

NC = 8192
PANELS = 4
CHILDREN = 4
CAPC = 2
RTD = 8
BLK = 128
GRAM_SLOTS = 5
FIRST = 3
CHUNKS = 2
CHOL_COST = 200 << 30
HIGHEST = lax.Precision.HIGHEST
F32 = jnp.float32
BF16 = jnp.bfloat16
VMEM_LIMIT = 56 << 20


def split(x):
    high = x.astype(BF16)
    return high, (x - high.astype(F32)).astype(BF16)


def dot3(a_high, a_low, b_high, b_low):
    left = jnp.concatenate([a_high, a_high, a_low], axis=1)
    right = jnp.concatenate([b_high, b_low, b_high], axis=0)
    return jnp.dot(left, right, preferred_element_type=F32)


def params():
    return pltpu.CompilerParams(vmem_limit_bytes=VMEM_LIMIT)


def take_groups(tiles, picks):
    (groups, count), (high, wide) = picks.shape, tiles.shape[1:]

    def kernel(pick_ref, *refs):
        for in_ref, out_ref in zip(refs[:groups], refs[groups:]):
            out_ref[...] = in_ref[...]

    return pl.pallas_call(
        kernel,
        grid_spec=pltpu.PrefetchScalarGridSpec(
            num_scalar_prefetch=1,
            grid=(count,),
            in_specs=[
                pl.BlockSpec((1, high, wide), lambda i, pick, g=g: (pick[g * count + i], 0, 0)) for g in range(groups)
            ],
            out_specs=[pl.BlockSpec((1, high, wide), lambda i, pick: (i, 0, 0))] * groups,
        ),
        out_shape=[jax.ShapeDtypeStruct((count, high, wide), F32)] * groups,
        cost_estimate=pl.CostEstimate(flops=0, bytes_accessed=8 * groups * count * high * wide, transcendentals=0),
        name="take_groups",
    )(picks.reshape(-1), *[tiles] * groups)


def take_leads(tiles, picks, note):
    count, (high, wide), extra = picks.shape[0], tiles.shape[1:], note.shape[0]

    def kernel(pick_ref, in_ref, note_ref, out_ref):
        out_ref[0, :high] = in_ref[0]
        out_ref[0, high:] = note_ref[...]

    return pl.pallas_call(
        kernel,
        grid_spec=pltpu.PrefetchScalarGridSpec(
            num_scalar_prefetch=1,
            grid=(count,),
            in_specs=[
                pl.BlockSpec((1, high, wide), lambda i, pick: (pick[i], 0, 0)),
                pl.BlockSpec((extra, wide), lambda i, pick: (0, 0)),
            ],
            out_specs=pl.BlockSpec((1, high + extra, wide), lambda i, pick: (i, 0, 0)),
        ),
        out_shape=jax.ShapeDtypeStruct((count, high + extra, wide), F32),
        cost_estimate=pl.CostEstimate(flops=0, bytes_accessed=8 * count * high * wide, transcendentals=0),
        name="take_leads",
    )(picks, tiles, note)


def gram_table(col_count):
    blocks = col_count
    table = []
    for c in range(col_count):
        low = min(c, blocks - 1 - c)
        shared = [(i, j) for i in (low, blocks - 1 - low) for j in range(i, blocks)]
        mine = shared[::2] if c == low else shared[1::2]
        table.append((mine + mine[-1:])[: GRAM_SLOTS])
    return table


def place_leads(pos_ref, lead_refs, sum_ref, transposed):
    sum_ref[...] = jnp.zeros_like(sum_ref)
    count, size = lead_refs[0].shape[0], lead_refs[0].shape[2]
    for s, ref in enumerate(lead_refs):

        def place(r, _, s=s, ref=ref):
            pos = pos_ref[s * count + r]

            @pl.when(pos >= 0)
            def _():
                at_row = pl.ds(pl.multiple_of((pos // PANELS) * size, size), size)
                at_col = pl.ds(pl.multiple_of((pos % PANELS) * size, size), size)
                if transposed:
                    sum_ref[at_col, at_row] += ref[r, :size].T
                else:
                    sum_ref[at_row, at_col] += ref[r, :size]

            return 0

        lax.fori_loop(0, count, place, 0)


def gram_slice(mine, positions, leads):
    size = leads[0].shape[2]
    width, depth = PANELS * size, RTD * size

    def kernel(mine_ref, pos_ref, *refs):
        lead_refs, (out_ref, sum_ref, left_ref) = refs[: len(leads)], refs[len(leads) :]
        place_leads(pos_ref, lead_refs, sum_ref, False)

        def block(s, _):
            at_i = pl.ds(pl.multiple_of(mine_ref[2 * s] * BLK, BLK), BLK)
            at_j = pl.ds(pl.multiple_of(mine_ref[2 * s + 1] * BLK, BLK), BLK)
            at_s = pl.ds(pl.multiple_of(s * BLK, BLK), BLK)
            for k in range(RTD):
                rows = slice(k * size, (k + 1) * size)
                left_ref[:, rows] = sum_ref[rows, at_i].T
            a_high, a_low = split(left_ref[...])
            b_high, b_low = split(sum_ref[:, at_j])
            block_out = dot3(a_high, a_low, b_high, b_low)
            for g in range(BLK // 8):
                out_ref[g, :, at_s] = block_out[8 * g : 8 * g + 8]
            return 0

        lax.fori_loop(0, GRAM_SLOTS, block, 0)

    smem = pl.BlockSpec(memory_space=pltpu.SMEM)
    vmem = pl.BlockSpec(memory_space=pltpu.VMEM)
    return pl.pallas_call(
        kernel,
        in_specs=[smem, smem] + [vmem] * len(leads),
        out_specs=vmem,
        out_shape=jax.ShapeDtypeStruct((BLK // 8, 8, GRAM_SLOTS * BLK), F32),
        scratch_shapes=[pltpu.VMEM((depth, width), F32), pltpu.VMEM((BLK, depth), F32)],
        compiler_params=params(),
        cost_estimate=pl.CostEstimate(
            flops=6 * BLK * width * depth, bytes_accessed=4 * 16 * size * size, transcendentals=0
        ),
        name="gram_slice",
    )(mine, positions, *leads)


def leading_split(positions, leads):
    size = leads[0].shape[2]
    width, depth = PANELS * size, RTD * size

    def kernel(pos_ref, *refs):
        lead_refs, (high_ref, low_ref, sum_ref) = refs[: len(leads)], refs[len(leads) :]
        place_leads(pos_ref, lead_refs, sum_ref, True)

        def step(k, _):
            rows = pl.ds(pl.multiple_of(k * BLK, BLK), BLK)
            high_ref[rows, :], low_ref[rows, :] = split(sum_ref[rows, :])
            return 0

        lax.fori_loop(0, width // BLK, step, 0)

    smem = pl.BlockSpec(memory_space=pltpu.SMEM)
    vmem = pl.BlockSpec(memory_space=pltpu.VMEM)
    return pl.pallas_call(
        kernel,
        in_specs=[smem] + [vmem] * len(leads),
        out_specs=[vmem, vmem],
        out_shape=[jax.ShapeDtypeStruct((width, depth), BF16)] * 2,
        scratch_shapes=[pltpu.VMEM((width, depth), F32)],
        compiler_params=params(),
        cost_estimate=pl.CostEstimate(flops=0, bytes_accessed=12 << 20, transcendentals=0),
        name="leading_split",
    )(positions, *leads)


def cross_products(positions, groups, lead_high, lead_low):
    width, depth = lead_high.shape
    size = groups[0][0][0].shape[-2]
    chunks = len(groups[0][0])
    count = len(groups) * CAPC
    step = 256

    def kernel(pos_ref, *refs):
        tile_refs, (high_ref, low_ref, out_ref) = refs[: len(groups) * chunks], refs[len(groups) * chunks :]
        out_ref[...] = jnp.zeros_like(out_ref)
        for g in range(len(groups)):
            parts = tile_refs[g * chunks : (g + 1) * chunks]

            def place(i, _, parts=parts, first=g * CAPC):
                pos = pos_ref[first + i]

                @pl.when(pos >= 0)
                def _():
                    at_row = pl.ds(pl.multiple_of((pos // PANELS) * size, size), size)
                    at_col = pl.ds(pl.multiple_of((pos % PANELS) * size, size), size)
                    b_high, b_low = split(jnp.concatenate([ref[0, i] for ref in parts], axis=1))
                    dot = lambda x, y: jnp.dot(x, y, preferred_element_type=F32)
                    for m in range(0, width, step):
                        a_high, a_low = high_ref[m : m + step, at_row], low_ref[m : m + step, at_row]
                        out_ref[m : m + step, at_col] += dot(a_high, b_high) + dot(a_high, b_low) + dot(a_low, b_high)

                return 0

            lax.fori_loop(0, CAPC, place, 0)

    return pl.pallas_call(
        kernel,
        grid_spec=pltpu.PrefetchScalarGridSpec(
            num_scalar_prefetch=1,
            grid=(1,),
            in_specs=[
                pl.BlockSpec((1, *v.shape[1:]), lambda i, pos, n=n: (n, 0, 0, 0), pipeline_mode=pl.Buffered(1))
                for vs, n in groups
                for v in vs
            ]
            + [pl.BlockSpec((width, depth), lambda i, pos: (0, 0), pipeline_mode=pl.Buffered(1))] * 2,
            out_specs=pl.BlockSpec((width, PANELS * size), lambda i, pos: (0, 0), pipeline_mode=pl.Buffered(1)),
        ),
        out_shape=jax.ShapeDtypeStruct((width, PANELS * size), F32),
        compiler_params=params(),
        cost_estimate=pl.CostEstimate(
            flops=6 * count * width * size * size, bytes_accessed=16 << 20, transcendentals=0
        ),
        name="cross_products",
    )(positions, *[v for vs, _ in groups for v in vs], lead_high, lead_low)


def block_factor(block):
    tiles = BLK // 8
    lane = lax.broadcasted_iota(jnp.int32, (8, BLK), 1)
    sub = lax.broadcasted_iota(jnp.int32, (8, BLK), 0)
    full = lambda v: jnp.broadcast_to(v, (8, BLK))
    x = [block[8 * t : 8 * t + 8, :] for t in range(tiles)]
    out = []
    for t in range(tiles):
        base = 8 * t
        panel = lane // 8 == t
        rows = [full(x[t][p : p + 1, :]) for p in range(8)]
        a = {(p, q): full(rows[p][:, base + q : base + q + 1]) for p in range(8) for q in range(p, 8)}
        rows = [jnp.where(panel, jnp.where(lane == base + p, 1.0, 0.0), rows[p]) for p in range(8)]
        columns = {u: [full(x[u][:, base + p : base + p + 1]) for p in range(8)] for u in range(t + 1, tiles)}
        for u in range(t + 1, tiles):
            x[u] = jnp.where(panel, 0.0, x[u])
        scales = []
        for p in range(8):
            inverse = 1.0 / a[p, p]
            scale = lax.rsqrt(a[p, p])
            scales.append(scale * (1.5 - 0.5 * a[p, p] * scale * scale))
            scaled = rows[p] * inverse
            ratio = [a[p, q] * inverse for q in range(p + 1, 8)]
            for q in range(p + 1, 8):
                for r in range(q, 8):
                    a[q, r] = a[q, r] - a[p, q] * ratio[r - p - 1]
                rows[q] = rows[q] - a[p, q] * scaled
            for u in range(t + 1, tiles):
                for q in range(p + 1, 8):
                    columns[u][q] = columns[u][q] - columns[u][p] * ratio[q - p - 1]
                x[u] = x[u] - columns[u][p] * scaled
        tile = rows[0] * scales[0]
        for p in range(1, 8):
            tile = jnp.where(sub == p, rows[p] * scales[p], tile)
        out.append(jnp.where(lane <= sub + base, tile, 0.0))
    return jnp.concatenate(out, axis=0)


def eliminate(first, last, work_ref, out_ref, row_ref):
    width = work_ref.shape[1]

    def outer(k, _):
        at = pl.multiple_of(k * BLK, BLK)
        here = pl.ds(at, BLK)
        inverse = block_factor(work_ref[here, here])
        row_ref[...] = jnp.dot(inverse, work_ref[here, :], precision=HIGHEST, preferred_element_type=F32)
        row_ref[:, here] = inverse
        row = row_ref[...]
        lane = lax.broadcasted_iota(jnp.int32, (BLK, width), 1)
        out_ref[pl.ds(pl.multiple_of(at - first * BLK, BLK), BLK), :] = jnp.where(lane < at + BLK, row, 0.0)

        def inner(i, _):
            below = pl.ds(pl.multiple_of(i * BLK, BLK), BLK)
            factor = row_ref[:, below].T
            work_ref[below, here] = jnp.zeros((BLK, BLK), F32)
            work_ref[below, :] -= jnp.dot(factor, row, precision=HIGHEST, preferred_element_type=F32)
            return 0

        lax.fori_loop(k + 1, width // BLK, inner, 0)
        return 0

    lax.fori_loop(first, last, outer, 0)


def inverse_cholesky_start(spots, parts, width):
    def kernel(spot_ref, *refs):
        part_refs, (out_ref, rest_ref, work_ref, row_ref) = refs[: len(parts)], refs[len(parts) :]
        for n, ref in enumerate(part_refs):
            count = ref.shape[0]

            def fill(s, _, n=n, ref=ref, count=count):
                q, r = s // GRAM_SLOTS, s % GRAM_SLOTS
                at = 2 * (n * count * GRAM_SLOTS + s)
                row = pl.multiple_of(spot_ref[at] * BLK, BLK)
                col = pl.multiple_of(spot_ref[at + 1] * BLK, BLK)
                lanes = pl.ds(pl.multiple_of(r * BLK, BLK), BLK)
                for g in range(BLK // 8):
                    work_ref[pl.ds(row + 8 * g, 8), pl.ds(col, BLK)] = ref[q, g, :, lanes]
                return 0

            lax.fori_loop(0, count * GRAM_SLOTS, fill, 0)
        eliminate(0, FIRST, work_ref, out_ref, row_ref)
        rest_ref[...] = work_ref[FIRST * BLK :, :]

    smem = pl.BlockSpec(memory_space=pltpu.SMEM)
    vmem = pl.BlockSpec(memory_space=pltpu.VMEM)
    return pl.pallas_call(
        kernel,
        in_specs=[smem] + [vmem] * len(parts),
        out_specs=[vmem, vmem],
        out_shape=[
            jax.ShapeDtypeStruct((FIRST * BLK, width), F32),
            jax.ShapeDtypeStruct((width - FIRST * BLK, width), F32),
        ],
        scratch_shapes=[pltpu.VMEM((width, width), F32), pltpu.VMEM((BLK, width), F32)],
        compiler_params=params(),
        cost_estimate=pl.CostEstimate(flops=CHOL_COST, bytes_accessed=8 << 20, transcendentals=0),
        name="inverse_cholesky_start",
    )(spots, *parts)


def inverse_cholesky_end(rest):
    low, width = rest.shape
    first = (width - low) // BLK

    def kernel(rest_ref, out_ref, work_ref, row_ref):
        work_ref[first * BLK :, :] = rest_ref[...]
        eliminate(first, width // BLK, work_ref, out_ref, row_ref)

    vmem = pl.BlockSpec(memory_space=pltpu.VMEM)
    return pl.pallas_call(
        kernel,
        in_specs=[vmem],
        out_specs=vmem,
        out_shape=jax.ShapeDtypeStruct((low, width), F32),
        scratch_shapes=[pltpu.VMEM((width, width), F32), pltpu.VMEM((BLK, width), F32)],
        compiler_params=params(),
        cost_estimate=pl.CostEstimate(flops=CHOL_COST, bytes_accessed=8 << 20, transcendentals=0),
        name="inverse_cholesky_end",
    )(rest)


def solved_rows(col_here, inverses, crosses):
    width, cols = crosses[0].shape[0], sum(c.shape[1] for c in crosses)
    wide = crosses[0].shape[1] // PANELS
    size = wide * len(crosses)

    def kernel(col_ref, *refs):
        inv_refs, refs = refs[: len(inverses)], refs[len(inverses) :]
        cross_refs, (out_ref, high_ref, low_ref) = refs[: len(crosses)], refs[len(crosses) :]
        i = pl.program_id(0)

        @pl.when(i == 0)
        def _():
            at = 0
            for ref in inv_refs:
                rows = slice(at, at + ref.shape[0])
                high_ref[rows, :], low_ref[rows, :] = split(ref[...])
                at += ref.shape[0]

        b_high, b_low = split(jnp.concatenate([ref[...] for ref in cross_refs], axis=1))
        first = col_ref[0] * cols + i * size
        step = 256
        for k in range(width // step):
            rows, done = slice(k * step, (k + 1) * step), (k + 1) * step
            value = dot3(high_ref[rows, :done], low_ref[rows, :done], b_high[:done], b_low[:done])
            row = lax.broadcasted_iota(jnp.int32, (step, size), 0) + k * step
            col = lax.broadcasted_iota(jnp.int32, (step, size), 1) + first
            out_ref[rows, :] = jnp.where(col >= row, value, 0.0)

    return pl.pallas_call(
        kernel,
        grid_spec=pltpu.PrefetchScalarGridSpec(
            num_scalar_prefetch=1,
            grid=(cols // size,),
            in_specs=[
                pl.BlockSpec(part.shape, lambda i, col: (0, 0), pipeline_mode=pl.Buffered(1)) for part in inverses
            ]
            + [pl.BlockSpec((width, wide), lambda i, col: (0, i))] * len(crosses),
            out_specs=pl.BlockSpec((width, size), lambda i, col: (0, i)),
            scratch_shapes=[pltpu.VMEM((width, width), BF16)] * 2,
        ),
        out_shape=jax.ShapeDtypeStruct((width, cols), F32),
        compiler_params=params(),
        cost_estimate=pl.CostEstimate(flops=6 * width * width * cols, bytes_accessed=12 << 20, transcendentals=0),
        name="solved_rows",
    )(col_here, *inverses, *crosses)


def rotated(amount, value, row_count):
    def by(shift):
        if shift == 0:
            return lambda v: v
        pairs = [(i, (i + shift) % row_count) for i in range(row_count)]
        return lambda v: lax.ppermute(v, "row", pairs)

    return lax.switch(amount, [by(k) for k in range(row_count)], value)


def step_pairs(step, col_count):
    half = col_count // 2
    return [(i, ((i // 2 + step) % half) * 2 + i % 2) for i in range(col_count)]


def pair_steps(value, col_count):
    return [value] + [lax.ppermute(value, "col", step_pairs(d, col_count)) for d in range(1, col_count // 2)]


def both_cores(own, col_count):
    own = jnp.stack(own)
    return own, lax.ppermute(own, "col", [(i, i ^ 1) for i in range(col_count)])


def exchanged(parts, axis):
    return lax.all_to_all(parts, axis, split_axis=0, concat_axis=0, tiled=True)


def summed_rows(parts):
    own = jnp.sum(exchanged(parts, "row"), axis=0)
    return exchanged(jnp.broadcast_to(own[None], parts.shape), "row")


def shards(child_tiles, tile_dest, tile_counts, child_offsets):
    row_count = lax.axis_size("row")
    col_count = lax.axis_size("col")
    row_here = lax.axis_index("row")
    col_here = lax.axis_index("col")
    slot_count, size = child_tiles.shape[:2]
    tiles_col = NC // col_count // size
    width = PANELS * size
    slots = jnp.arange(slot_count, dtype=jnp.int32)
    cols = jnp.arange(col_count, dtype=jnp.int32)
    child_of = cols // (col_count // CHILDREN)
    offsets = jnp.sum(jnp.where(child_of[:, None] == jnp.arange(CHILDREN)[None, :], child_offsets[None, :], 0), axis=1)
    offset_here = jnp.sum(jnp.where(cols == col_here, offsets, 0))
    amount = offset_here % row_count

    owner = jnp.where(slots < tile_counts[0, 0], tile_dest[:, 0] // tiles_col, -1)
    local_row = tile_dest[:, 1] + (offset_here + row_here) // row_count
    position = local_row * tiles_col + tile_dest[:, 0] % tiles_col
    earlier = (owner[:, None] == owner[None, :]) & (slots[None, :] < slots[:, None])
    bucket = jnp.where(owner >= 0, owner * CAPC + jnp.sum(earlier, axis=1), -1)
    hit = jnp.arange(col_count * CAPC, dtype=jnp.int32)[:, None] == bucket[None, :]
    picks = jnp.sum(jnp.where(hit, slots[None, :], 0), axis=1)
    places = jnp.sum(jnp.where(hit, position[None, :] + 1, 0), axis=1) - 1
    meta = jnp.concatenate([picks, places]).astype(jnp.int32)

    note = jnp.broadcast_to(jnp.pad(meta.astype(F32), (0, size - meta.shape[0])), (8, size))
    lead = rotated(amount, take_leads(child_tiles, picks[:CAPC].astype(jnp.int32), note), row_count)
    near = pair_steps(lead, col_count)
    my_picks = lead[0, size, : col_count * CAPC].astype(jnp.int32).reshape(col_count, CAPC)
    half = col_count // 2
    steps = jnp.arange(half)[:, None]
    targets = ((col_here // 2 + steps) % half) * 2 + (col_here + jnp.arange(2)[None, :]) % 2
    chosen = targets[:, :, None] == cols
    my_picks = jnp.sum(jnp.where(chosen[..., None], my_picks, 0), axis=2).reshape(half, 2 * CAPC)
    wide = size // CHUNKS
    far, stacks = [], None
    for c in range(CHUNKS):
        ready = child_tiles[:, :, c * wide : (c + 1) * wide]
        if c == 0:
            ready, _, my_picks = lax.optimization_barrier((ready, lead, my_picks))
        else:
            ready, _, _ = lax.optimization_barrier((ready, packed, stacks[0]))
        tiles = rotated(amount, ready, row_count)
        if c == 0:
            near, tiles = lax.optimization_barrier((near, tiles))
            stacks = both_cores(near, col_count)
        else:
            far, tiles = lax.optimization_barrier((far, tiles))
        packed = [v.reshape(2, CAPC, size, wide) for v in take_groups(tiles, my_picks)]
        if c == CHUNKS - 1:
            stacks, packed = lax.optimization_barrier((stacks, packed))
        far.append([packed[0]] + [lax.ppermute(packed[d], "col", step_pairs(d, col_count)) for d in range(1, half)])

    notes = jnp.concatenate([v[:, 0, size, : meta.shape[0]] for v in stacks]).astype(jnp.int32)
    places = notes[:, col_count * CAPC :].reshape(col_count, col_count, CAPC)
    lead_places = places[:, 0].reshape(-1)
    order = jnp.stack([((col_here // 2 - d) % half) * 2 + (col_here + c) % 2 for c in range(2) for d in range(half)])
    ordered = order[:, None] == cols[None, :]
    my_places = jnp.sum(jnp.where(cols[None, :, None] == col_here, places, 0), axis=1).reshape(-1)
    table = jnp.array(gram_table(col_count), jnp.int32).reshape(col_count, -1)
    spots = jnp.sum(jnp.where(ordered[:, :, None], table[None], 0), axis=1)
    col_scalar = col_here.reshape(1).astype(jnp.int32)

    leads = [v.reshape(-1, *v.shape[2:]) for v in stacks]
    gram_part = summed_rows(gram_slice(spots[0], lead_places, leads))
    swap = [(i, i ^ 1) for i in range(col_count)]
    lead_high, lead_low = leading_split(lead_places, leads)
    others = [[lax.ppermute(v, "col", swap) for v in chunk] for chunk in far[:-1]]
    far, gram_part, lead_high, lead_low = lax.optimization_barrier((far, gram_part, lead_high, lead_low))
    others.append([lax.ppermute(v, "col", swap) for v in far[-1]])
    others, gram_part = lax.optimization_barrier((others, gram_part))
    gram_near = pair_steps(gram_part, col_count)
    groups = [(v, 0) for v in zip(*far)] + [(v, 1) for v in zip(*others)]
    cross = cross_products(my_places, groups, lead_high, lead_low)
    gram_near, cross = lax.optimization_barrier((gram_near, cross))
    gram_parts, cross = lax.optimization_barrier((both_cores(gram_near, col_count), cross))
    cross = summed_rows(cross.reshape(row_count, width // row_count, -1)).reshape(width, -1)
    begun, rest = inverse_cholesky_start(spots.reshape(-1), gram_parts, width)
    ended = inverse_cholesky_end(rest)
    return solved_rows(col_scalar, [begun, ended], [cross])


def solution(mesh):
    return jax.shard_map(
        shards,
        mesh=mesh,
        in_specs=(P(("row", "col"), None, None), P(("row", "col"), None), P("row", "col"), P()),
        out_specs=P(None, "col"),
        check_vma=False,
    )
```

```python
import jax
import jax.numpy as jnp
from jax import lax
from jax.experimental import pallas as pl
from jax.experimental.pallas import tpu as pltpu
from jax.sharding import PartitionSpec as P

NC = 8192
PANELS = 4
CHILDREN = 4
CAPC = 2
RTD = 8
BLK = 128
NOTE = 8
GRAM_SLOTS = 5
FIRST = 3
CHUNKS = 2
CHOL_COST = 200 << 30
HIGHEST = lax.Precision.HIGHEST
F32 = jnp.float32
BF16 = jnp.bfloat16
VMEM_LIMIT = 56 << 20


def split(x):
    high = x.astype(BF16)
    return high, (x - high.astype(F32)).astype(BF16)


def dot3(a_high, a_low, b_high, b_low):
    left = jnp.concatenate([a_high, a_high, a_low], axis=1)
    right = jnp.concatenate([b_high, b_low, b_high], axis=0)
    return jnp.dot(left, right, preferred_element_type=F32)


def params():
    return pltpu.CompilerParams(vmem_limit_bytes=VMEM_LIMIT)


def take_groups(tiles, picks):
    (groups, count), (high, wide) = picks.shape, tiles.shape[1:]

    def kernel(pick_ref, *refs):
        for in_ref, out_ref in zip(refs[:groups], refs[groups:]):
            out_ref[...] = in_ref[...]

    return pl.pallas_call(
        kernel,
        grid_spec=pltpu.PrefetchScalarGridSpec(
            num_scalar_prefetch=1,
            grid=(count,),
            in_specs=[
                pl.BlockSpec((1, high, wide), lambda i, pick, g=g: (pick[g * count + i], 0, 0)) for g in range(groups)
            ],
            out_specs=[pl.BlockSpec((1, high, wide), lambda i, pick: (i, 0, 0))] * groups,
        ),
        out_shape=[jax.ShapeDtypeStruct((count, high, wide), F32)] * groups,
        cost_estimate=pl.CostEstimate(flops=0, bytes_accessed=8 * groups * count * high * wide, transcendentals=0),
        name="take_groups",
    )(picks.reshape(-1), *[tiles] * groups)


def take_leads(tiles, dest, counts, offsets, cols, row_count):
    slot_count, high, wide = tiles.shape
    buckets = cols * CAPC

    def kernel(dest_ref, count_ref, offset_ref, tile_ref, out_ref, meta_ref, note_ref, sems):
        col = lax.axis_index("col")
        base = (offset_ref[col // (cols // CHILDREN)] + lax.axis_index("row")) // row_count
        for i in range(buckets):
            meta_ref[i] = 0
            meta_ref[buckets + i] = -1
        tiles_col = NC // cols // wide
        for s in range(slot_count):
            first = dest_ref[s, 0] // tiles_col * CAPC

            @pl.when(s < count_ref[0, 0])
            def _(s=s, first=first):
                at = first + jnp.where(meta_ref[buckets + first] >= 0, 1, 0)
                meta_ref[at] = s
                meta_ref[buckets + at] = (dest_ref[s, 1] + base) * tiles_col + dest_ref[s, 0] % tiles_col

        copies = [
            pltpu.make_async_copy(tile_ref.at[meta_ref[r]], out_ref.at[r, pl.ds(0, high)], sems.at[r]) for r in range(CAPC)
        ]
        for copy in copies:
            copy.start()
        lane = lax.broadcasted_iota(jnp.int32, note_ref.shape, 1)
        note = jnp.zeros(note_ref.shape, jnp.int32)
        for i in range(2 * buckets):
            note = jnp.where(lane == i, meta_ref[i], note)
        note_ref[...] = note.astype(F32)
        more = [
            pltpu.make_async_copy(note_ref, out_ref.at[r, pl.ds(high, NOTE)], sems.at[CAPC + r]) for r in range(CAPC)
        ]
        for copy in more:
            copy.start()
        for copy in copies + more:
            copy.wait()

    smem = pl.BlockSpec(memory_space=pltpu.SMEM)
    return pl.pallas_call(
        kernel,
        in_specs=[smem, smem, smem, pl.BlockSpec(memory_space=pl.ANY)],
        out_specs=pl.BlockSpec(memory_space=pl.ANY),
        out_shape=jax.ShapeDtypeStruct((CAPC, high + NOTE, wide), F32),
        scratch_shapes=[
            pltpu.SMEM((2 * buckets,), jnp.int32),
            pltpu.VMEM((NOTE, wide), F32),
            pltpu.SemaphoreType.DMA((2 * CAPC,)),
        ],
        cost_estimate=pl.CostEstimate(flops=0, bytes_accessed=8 * CAPC * high * wide, transcendentals=0),
        name="take_leads",
    )(dest, counts, offsets, tiles)


def gram_table(col_count):
    blocks = col_count
    table = []
    for c in range(col_count):
        low = min(c, blocks - 1 - c)
        shared = [(i, j) for i in (low, blocks - 1 - low) for j in range(i, blocks)]
        mine = shared[::2] if c == low else shared[1::2]
        table.append((mine + mine[-1:])[: GRAM_SLOTS])
    return table


def place_leads(pos_ref, lead_refs, sum_ref, transposed):
    sum_ref[...] = jnp.zeros_like(sum_ref)
    count, size = lead_refs[0].shape[0], lead_refs[0].shape[2]
    for s, ref in enumerate(lead_refs):

        def place(r, _, s=s, ref=ref):
            pos = pos_ref[s * count + r]

            @pl.when(pos >= 0)
            def _():
                at_row = pl.ds(pl.multiple_of((pos // PANELS) * size, size), size)
                at_col = pl.ds(pl.multiple_of((pos % PANELS) * size, size), size)
                if transposed:
                    sum_ref[at_col, at_row] += ref[r, :size].T
                else:
                    sum_ref[at_row, at_col] += ref[r, :size]

            return 0

        lax.fori_loop(0, count, place, 0)


def gram_slice(mine, positions, leads):
    size = leads[0].shape[2]
    width, depth = PANELS * size, RTD * size

    def kernel(mine_ref, pos_ref, *refs):
        lead_refs, (out_ref, sum_ref, left_ref) = refs[: len(leads)], refs[len(leads) :]
        place_leads(pos_ref, lead_refs, sum_ref, False)

        def block(s, _):
            at_i = pl.ds(pl.multiple_of(mine_ref[2 * s] * BLK, BLK), BLK)
            at_j = pl.ds(pl.multiple_of(mine_ref[2 * s + 1] * BLK, BLK), BLK)
            at_s = pl.ds(pl.multiple_of(s * BLK, BLK), BLK)
            for k in range(RTD):
                rows = slice(k * size, (k + 1) * size)
                left_ref[:, rows] = sum_ref[rows, at_i].T
            a_high, a_low = split(left_ref[...])
            b_high, b_low = split(sum_ref[:, at_j])
            block_out = dot3(a_high, a_low, b_high, b_low)
            for g in range(BLK // 8):
                out_ref[g, :, at_s] = block_out[8 * g : 8 * g + 8]
            return 0

        lax.fori_loop(0, GRAM_SLOTS, block, 0)

    smem = pl.BlockSpec(memory_space=pltpu.SMEM)
    vmem = pl.BlockSpec(memory_space=pltpu.VMEM)
    return pl.pallas_call(
        kernel,
        in_specs=[smem, smem] + [vmem] * len(leads),
        out_specs=vmem,
        out_shape=jax.ShapeDtypeStruct((BLK // 8, 8, GRAM_SLOTS * BLK), F32),
        scratch_shapes=[pltpu.VMEM((depth, width), F32), pltpu.VMEM((BLK, depth), F32)],
        compiler_params=params(),
        cost_estimate=pl.CostEstimate(
            flops=6 * BLK * width * depth, bytes_accessed=4 * 16 * size * size, transcendentals=0
        ),
        name="gram_slice",
    )(mine, positions, *leads)


def leading_split(positions, leads):
    size = leads[0].shape[2]
    width, depth = PANELS * size, RTD * size

    def kernel(pos_ref, *refs):
        lead_refs, (high_ref, low_ref, sum_ref) = refs[: len(leads)], refs[len(leads) :]
        place_leads(pos_ref, lead_refs, sum_ref, True)

        def step(k, _):
            rows = pl.ds(pl.multiple_of(k * BLK, BLK), BLK)
            high_ref[rows, :], low_ref[rows, :] = split(sum_ref[rows, :])
            return 0

        lax.fori_loop(0, width // BLK, step, 0)

    smem = pl.BlockSpec(memory_space=pltpu.SMEM)
    vmem = pl.BlockSpec(memory_space=pltpu.VMEM)
    return pl.pallas_call(
        kernel,
        in_specs=[smem] + [vmem] * len(leads),
        out_specs=[vmem, vmem],
        out_shape=[jax.ShapeDtypeStruct((width, depth), BF16)] * 2,
        scratch_shapes=[pltpu.VMEM((width, depth), F32)],
        compiler_params=params(),
        cost_estimate=pl.CostEstimate(flops=0, bytes_accessed=12 << 20, transcendentals=0),
        name="leading_split",
    )(positions, *leads)


def cross_products(positions, groups, lead_high, lead_low):
    width, depth = lead_high.shape
    size = groups[0][0][0].shape[-2]
    chunks = len(groups[0][0])
    count = len(groups) * CAPC
    step = 256

    def kernel(pos_ref, *refs):
        tile_refs, (high_ref, low_ref, out_ref) = refs[: len(groups) * chunks], refs[len(groups) * chunks :]
        out_ref[...] = jnp.zeros_like(out_ref)
        for g in range(len(groups)):
            parts = tile_refs[g * chunks : (g + 1) * chunks]

            def place(i, _, parts=parts, first=g * CAPC):
                pos = pos_ref[first + i]

                @pl.when(pos >= 0)
                def _():
                    at_row = pl.ds(pl.multiple_of((pos // PANELS) * size, size), size)
                    at_col = pl.ds(pl.multiple_of((pos % PANELS) * size, size), size)
                    b_high, b_low = split(jnp.concatenate([ref[0, i] for ref in parts], axis=1))
                    dot = lambda x, y: jnp.dot(x, y, preferred_element_type=F32)
                    for m in range(0, width, step):
                        a_high, a_low = high_ref[m : m + step, at_row], low_ref[m : m + step, at_row]
                        out_ref[m : m + step, at_col] += dot(a_high, b_high) + dot(a_high, b_low) + dot(a_low, b_high)

                return 0

            lax.fori_loop(0, CAPC, place, 0)

    return pl.pallas_call(
        kernel,
        grid_spec=pltpu.PrefetchScalarGridSpec(
            num_scalar_prefetch=1,
            grid=(1,),
            in_specs=[
                pl.BlockSpec((1, *v.shape[1:]), lambda i, pos, n=n: (n, 0, 0, 0), pipeline_mode=pl.Buffered(1))
                for vs, n in groups
                for v in vs
            ]
            + [pl.BlockSpec((width, depth), lambda i, pos: (0, 0), pipeline_mode=pl.Buffered(1))] * 2,
            out_specs=pl.BlockSpec((width, PANELS * size), lambda i, pos: (0, 0), pipeline_mode=pl.Buffered(1)),
        ),
        out_shape=jax.ShapeDtypeStruct((width, PANELS * size), F32),
        compiler_params=params(),
        cost_estimate=pl.CostEstimate(
            flops=6 * count * width * size * size, bytes_accessed=16 << 20, transcendentals=0
        ),
        name="cross_products",
    )(positions, *[v for vs, _ in groups for v in vs], lead_high, lead_low)


def block_factor(block):
    tiles = BLK // 8
    lane = lax.broadcasted_iota(jnp.int32, (8, BLK), 1)
    sub = lax.broadcasted_iota(jnp.int32, (8, BLK), 0)
    full = lambda v: jnp.broadcast_to(v, (8, BLK))
    x = [block[8 * t : 8 * t + 8, :] for t in range(tiles)]
    out = []
    for t in range(tiles):
        base = 8 * t
        panel = lane // 8 == t
        rows = [full(x[t][p : p + 1, :]) for p in range(8)]
        a = {(p, q): full(rows[p][:, base + q : base + q + 1]) for p in range(8) for q in range(p, 8)}
        rows = [jnp.where(panel, jnp.where(lane == base + p, 1.0, 0.0), rows[p]) for p in range(8)]
        columns = {u: [full(x[u][:, base + p : base + p + 1]) for p in range(8)] for u in range(t + 1, tiles)}
        for u in range(t + 1, tiles):
            x[u] = jnp.where(panel, 0.0, x[u])
        scales = []
        for p in range(8):
            inverse = 1.0 / a[p, p]
            scale = lax.rsqrt(a[p, p])
            scales.append(scale * (1.5 - 0.5 * a[p, p] * scale * scale))
            scaled = rows[p] * inverse
            ratio = [a[p, q] * inverse for q in range(p + 1, 8)]
            for q in range(p + 1, 8):
                for r in range(q, 8):
                    a[q, r] = a[q, r] - a[p, q] * ratio[r - p - 1]
                rows[q] = rows[q] - a[p, q] * scaled
            for u in range(t + 1, tiles):
                for q in range(p + 1, 8):
                    columns[u][q] = columns[u][q] - columns[u][p] * ratio[q - p - 1]
                x[u] = x[u] - columns[u][p] * scaled
        tile = rows[0] * scales[0]
        for p in range(1, 8):
            tile = jnp.where(sub == p, rows[p] * scales[p], tile)
        out.append(jnp.where(lane <= sub + base, tile, 0.0))
    return jnp.concatenate(out, axis=0)


def eliminate(first, last, work_ref, out_ref, row_ref):
    width = work_ref.shape[1]

    def outer(k, _):
        at = pl.multiple_of(k * BLK, BLK)
        here = pl.ds(at, BLK)
        inverse = block_factor(work_ref[here, here])
        row_ref[...] = jnp.dot(inverse, work_ref[here, :], precision=HIGHEST, preferred_element_type=F32)
        row_ref[:, here] = inverse
        row = row_ref[...]
        lane = lax.broadcasted_iota(jnp.int32, (BLK, width), 1)
        out_ref[pl.ds(pl.multiple_of(at - first * BLK, BLK), BLK), :] = jnp.where(lane < at + BLK, row, 0.0)

        def inner(i, _):
            below = pl.ds(pl.multiple_of(i * BLK, BLK), BLK)
            factor = row_ref[:, below].T
            work_ref[below, here] = jnp.zeros((BLK, BLK), F32)
            work_ref[below, :] -= jnp.dot(factor, row, precision=HIGHEST, preferred_element_type=F32)
            return 0

        lax.fori_loop(k + 1, width // BLK, inner, 0)
        return 0

    lax.fori_loop(first, last, outer, 0)


def inverse_cholesky_start(spots, parts, width):
    def kernel(spot_ref, *refs):
        part_refs, (out_ref, rest_ref, work_ref, row_ref) = refs[: len(parts)], refs[len(parts) :]
        for n, ref in enumerate(part_refs):
            count = ref.shape[0]

            def fill(s, _, n=n, ref=ref, count=count):
                q, r = s // GRAM_SLOTS, s % GRAM_SLOTS
                at = 2 * (n * count * GRAM_SLOTS + s)
                row = pl.multiple_of(spot_ref[at] * BLK, BLK)
                col = pl.multiple_of(spot_ref[at + 1] * BLK, BLK)
                lanes = pl.ds(pl.multiple_of(r * BLK, BLK), BLK)
                for g in range(BLK // 8):
                    work_ref[pl.ds(row + 8 * g, 8), pl.ds(col, BLK)] = ref[q, g, :, lanes]
                return 0

            lax.fori_loop(0, count * GRAM_SLOTS, fill, 0)
        eliminate(0, FIRST, work_ref, out_ref, row_ref)
        rest_ref[...] = work_ref[FIRST * BLK :, :]

    smem = pl.BlockSpec(memory_space=pltpu.SMEM)
    vmem = pl.BlockSpec(memory_space=pltpu.VMEM)
    return pl.pallas_call(
        kernel,
        in_specs=[smem] + [vmem] * len(parts),
        out_specs=[vmem, vmem],
        out_shape=[
            jax.ShapeDtypeStruct((FIRST * BLK, width), F32),
            jax.ShapeDtypeStruct((width - FIRST * BLK, width), F32),
        ],
        scratch_shapes=[pltpu.VMEM((width, width), F32), pltpu.VMEM((BLK, width), F32)],
        compiler_params=params(),
        cost_estimate=pl.CostEstimate(flops=CHOL_COST, bytes_accessed=8 << 20, transcendentals=0),
        name="inverse_cholesky_start",
    )(spots, *parts)


def inverse_cholesky_end(rest):
    low, width = rest.shape
    first = (width - low) // BLK

    def kernel(rest_ref, out_ref, work_ref, row_ref):
        work_ref[first * BLK :, :] = rest_ref[...]
        eliminate(first, width // BLK, work_ref, out_ref, row_ref)

    vmem = pl.BlockSpec(memory_space=pltpu.VMEM)
    return pl.pallas_call(
        kernel,
        in_specs=[vmem],
        out_specs=vmem,
        out_shape=jax.ShapeDtypeStruct((low, width), F32),
        scratch_shapes=[pltpu.VMEM((width, width), F32), pltpu.VMEM((BLK, width), F32)],
        compiler_params=params(),
        cost_estimate=pl.CostEstimate(flops=CHOL_COST, bytes_accessed=8 << 20, transcendentals=0),
        name="inverse_cholesky_end",
    )(rest)


def solved_rows(col_here, inverses, crosses):
    width, cols = crosses[0].shape[0], sum(c.shape[1] for c in crosses)
    wide = crosses[0].shape[1] // PANELS
    size = wide * len(crosses)

    def kernel(col_ref, *refs):
        inv_refs, refs = refs[: len(inverses)], refs[len(inverses) :]
        cross_refs, (out_ref, high_ref, low_ref) = refs[: len(crosses)], refs[len(crosses) :]
        i = pl.program_id(0)

        @pl.when(i == 0)
        def _():
            at = 0
            for ref in inv_refs:
                rows = slice(at, at + ref.shape[0])
                high_ref[rows, :], low_ref[rows, :] = split(ref[...])
                at += ref.shape[0]

        b_high, b_low = split(jnp.concatenate([ref[...] for ref in cross_refs], axis=1))
        first = col_ref[0] * cols + i * size
        step = 256
        for k in range(width // step):
            rows, done = slice(k * step, (k + 1) * step), (k + 1) * step
            value = dot3(high_ref[rows, :done], low_ref[rows, :done], b_high[:done], b_low[:done])
            row = lax.broadcasted_iota(jnp.int32, (step, size), 0) + k * step
            col = lax.broadcasted_iota(jnp.int32, (step, size), 1) + first
            out_ref[rows, :] = jnp.where(col >= row, value, 0.0)

    return pl.pallas_call(
        kernel,
        grid_spec=pltpu.PrefetchScalarGridSpec(
            num_scalar_prefetch=1,
            grid=(cols // size,),
            in_specs=[
                pl.BlockSpec(part.shape, lambda i, col: (0, 0), pipeline_mode=pl.Buffered(1)) for part in inverses
            ]
            + [pl.BlockSpec((width, wide), lambda i, col: (0, i))] * len(crosses),
            out_specs=pl.BlockSpec((width, size), lambda i, col: (0, i)),
            scratch_shapes=[pltpu.VMEM((width, width), BF16)] * 2,
        ),
        out_shape=jax.ShapeDtypeStruct((width, cols), F32),
        compiler_params=params(),
        cost_estimate=pl.CostEstimate(flops=6 * width * width * cols, bytes_accessed=12 << 20, transcendentals=0),
        name="solved_rows",
    )(col_here, *inverses, *crosses)


def rotated(amount, value, row_count):
    def by(shift):
        if shift == 0:
            return lambda v: v
        pairs = [(i, (i + shift) % row_count) for i in range(row_count)]
        return lambda v: lax.ppermute(v, "row", pairs)

    return lax.switch(amount, [by(k) for k in range(row_count)], value)


def step_pairs(step, col_count):
    half = col_count // 2
    return [(i, ((i // 2 + step) % half) * 2 + i % 2) for i in range(col_count)]


def pair_steps(value, col_count):
    return [value] + [lax.ppermute(value, "col", step_pairs(d, col_count)) for d in range(1, col_count // 2)]


def both_cores(own, col_count):
    own = jnp.stack(own)
    return own, lax.ppermute(own, "col", [(i, i ^ 1) for i in range(col_count)])


def exchanged(parts, axis):
    return lax.all_to_all(parts, axis, split_axis=0, concat_axis=0, tiled=True)


def summed_rows(parts):
    own = jnp.sum(exchanged(parts, "row"), axis=0)
    return exchanged(jnp.broadcast_to(own[None], parts.shape), "row")


def shards(child_tiles, tile_dest, tile_counts, child_offsets):
    row_count = lax.axis_size("row")
    col_count = lax.axis_size("col")
    col_here = lax.axis_index("col")
    size = child_tiles.shape[1]
    width = PANELS * size
    cols = jnp.arange(col_count, dtype=jnp.int32)
    child_of = cols // (col_count // CHILDREN)
    offsets = jnp.sum(jnp.where(child_of[:, None] == jnp.arange(CHILDREN)[None, :], child_offsets[None, :], 0), axis=1)
    offset_here = jnp.sum(jnp.where(cols == col_here, offsets, 0))
    amount = offset_here % row_count

    taken = take_leads(child_tiles, tile_dest, tile_counts, child_offsets, col_count, row_count)
    lead = rotated(amount, taken, row_count)
    near = pair_steps(lead, col_count)
    my_picks = lead[0, size, : col_count * CAPC].astype(jnp.int32).reshape(col_count, CAPC)
    half = col_count // 2
    steps = jnp.arange(half)[:, None]
    targets = ((col_here // 2 + steps) % half) * 2 + (col_here + jnp.arange(2)[None, :]) % 2
    chosen = targets[:, :, None] == cols
    my_picks = jnp.sum(jnp.where(chosen[..., None], my_picks, 0), axis=2).reshape(half, 2 * CAPC)
    wide = size // CHUNKS
    far, stacks = [], None
    for c in range(CHUNKS):
        ready = child_tiles[:, :, c * wide : (c + 1) * wide]
        if c == 0:
            ready, _, my_picks = lax.optimization_barrier((ready, lead, my_picks))
        else:
            ready, _, _ = lax.optimization_barrier((ready, packed, stacks[0]))
        tiles = rotated(amount, ready, row_count)
        if c == 0:
            near, tiles = lax.optimization_barrier((near, tiles))
            stacks = both_cores(near, col_count)
        else:
            far, tiles = lax.optimization_barrier((far, tiles))
        packed = [v.reshape(2, CAPC, size, wide) for v in take_groups(tiles, my_picks)]
        if c == CHUNKS - 1:
            stacks, packed = lax.optimization_barrier((stacks, packed))
        far.append([packed[0]] + [lax.ppermute(packed[d], "col", step_pairs(d, col_count)) for d in range(1, half)])

    notes = jnp.concatenate([v[:, 0, size, : 2 * col_count * CAPC] for v in stacks]).astype(jnp.int32)
    places = notes[:, col_count * CAPC :].reshape(col_count, col_count, CAPC)
    lead_places = places[:, 0].reshape(-1)
    order = jnp.stack([((col_here // 2 - d) % half) * 2 + (col_here + c) % 2 for c in range(2) for d in range(half)])
    ordered = order[:, None] == cols[None, :]
    my_places = jnp.sum(jnp.where(cols[None, :, None] == col_here, places, 0), axis=1).reshape(-1)
    table = jnp.array(gram_table(col_count), jnp.int32).reshape(col_count, -1)
    spots = jnp.sum(jnp.where(ordered[:, :, None], table[None], 0), axis=1)
    col_scalar = col_here.reshape(1).astype(jnp.int32)

    leads = [v.reshape(-1, *v.shape[2:]) for v in stacks]
    gram_part = summed_rows(gram_slice(spots[0], lead_places, leads))
    swap = [(i, i ^ 1) for i in range(col_count)]
    lead_high, lead_low = leading_split(lead_places, leads)
    others = [[lax.ppermute(v, "col", swap) for v in chunk] for chunk in far[:-1]]
    far, gram_part, lead_high, lead_low = lax.optimization_barrier((far, gram_part, lead_high, lead_low))
    others.append([lax.ppermute(v, "col", swap) for v in far[-1]])
    others, gram_part = lax.optimization_barrier((others, gram_part))
    gram_near = pair_steps(gram_part, col_count)
    groups = [(v, 0) for v in zip(*far)] + [(v, 1) for v in zip(*others)]
    cross = cross_products(my_places, groups, lead_high, lead_low)
    gram_near, cross = lax.optimization_barrier((gram_near, cross))
    gram_parts, cross = lax.optimization_barrier((both_cores(gram_near, col_count), cross))
    cross = summed_rows(cross.reshape(row_count, width // row_count, -1)).reshape(width, -1)
    begun, rest = inverse_cholesky_start(spots.reshape(-1), gram_parts, width)
    ended = inverse_cholesky_end(rest)
    return solved_rows(col_scalar, [begun, ended], [cross])


def solution(mesh):
    return jax.shard_map(
        shards,
        mesh=mesh,
        in_specs=(P(("row", "col"), None, None), P(("row", "col"), None), P("row", "col"), P()),
        out_specs=P(None, "col"),
        check_vma=False,
    )
```

```python
import jax
import jax.numpy as jnp
from jax import lax
from jax.experimental import pallas as pl
from jax.experimental.pallas import tpu as pltpu
from jax.sharding import PartitionSpec as P

NC = 8192
PANELS = 4
CHILDREN = 4
CAPC = 2
RTD = 8
BLK = 128
NOTE = 8
GRAM_SLOTS = 5
FIRST = 3
CHUNKS = 2
CHOL_COST = 200 << 30
HIGHEST = lax.Precision.HIGHEST
F32 = jnp.float32
BF16 = jnp.bfloat16
VMEM_LIMIT = 56 << 20


def split(x):
    high = x.astype(BF16)
    return high, (x - high.astype(F32)).astype(BF16)


def dot3(a_high, a_low, b_high, b_low):
    left = jnp.concatenate([a_high, a_high, a_low], axis=1)
    right = jnp.concatenate([b_high, b_low, b_high], axis=0)
    return jnp.dot(left, right, preferred_element_type=F32)


def params():
    return pltpu.CompilerParams(vmem_limit_bytes=VMEM_LIMIT)


def take_groups(tiles, picks):
    (groups, count), (high, wide) = picks.shape, tiles.shape[1:]

    def kernel(pick_ref, *refs):
        for in_ref, out_ref in zip(refs[:groups], refs[groups:]):
            out_ref[...] = in_ref[...]

    return pl.pallas_call(
        kernel,
        grid_spec=pltpu.PrefetchScalarGridSpec(
            num_scalar_prefetch=1,
            grid=(count,),
            in_specs=[
                pl.BlockSpec((1, high, wide), lambda i, pick, g=g: (pick[g * count + i], 0, 0)) for g in range(groups)
            ],
            out_specs=[pl.BlockSpec((1, high, wide), lambda i, pick: (i, 0, 0))] * groups,
        ),
        out_shape=[jax.ShapeDtypeStruct((count, high, wide), F32)] * groups,
        cost_estimate=pl.CostEstimate(flops=0, bytes_accessed=8 * groups * count * high * wide, transcendentals=0),
        name="take_groups",
    )(picks.reshape(-1), *[tiles] * groups)


def take_leads(tiles, dest, counts, offsets, cols, row_count):
    slot_count, high, wide = tiles.shape
    buckets = cols * CAPC

    def kernel(dest_ref, count_ref, offset_ref, tile_ref, out_ref, meta_ref, note_ref, sems):
        col = lax.axis_index("col")
        base = (offset_ref[col // (cols // CHILDREN)] + lax.axis_index("row")) // row_count
        for i in range(buckets):
            meta_ref[i] = 0
            meta_ref[buckets + i] = -1
        tiles_col = NC // cols // wide
        for s in range(slot_count):
            first = dest_ref[s, 0] // tiles_col * CAPC

            @pl.when(s < count_ref[0, 0])
            def _(s=s, first=first):
                at = first + jnp.where(meta_ref[buckets + first] >= 0, 1, 0)
                meta_ref[at] = s
                meta_ref[buckets + at] = (dest_ref[s, 1] + base) * tiles_col + dest_ref[s, 0] % tiles_col

        copies = [
            pltpu.make_async_copy(tile_ref.at[meta_ref[r]], out_ref.at[r, pl.ds(0, high)], sems.at[r]) for r in range(CAPC)
        ]
        for copy in copies:
            copy.start()
        lane = lax.broadcasted_iota(jnp.int32, note_ref.shape, 1)
        note = jnp.zeros(note_ref.shape, jnp.int32)
        for i in range(2 * buckets):
            note = jnp.where(lane == i, meta_ref[i], note)
        note_ref[...] = note.astype(F32)
        more = [
            pltpu.make_async_copy(note_ref, out_ref.at[r, pl.ds(high, NOTE)], sems.at[CAPC + r]) for r in range(CAPC)
        ]
        for copy in more:
            copy.start()
        for copy in copies + more:
            copy.wait()

    smem = pl.BlockSpec(memory_space=pltpu.SMEM)
    return pl.pallas_call(
        kernel,
        in_specs=[smem, smem, smem, pl.BlockSpec(memory_space=pl.ANY)],
        out_specs=pl.BlockSpec(memory_space=pl.ANY),
        out_shape=jax.ShapeDtypeStruct((CAPC, high + NOTE, wide), F32),
        scratch_shapes=[
            pltpu.SMEM((2 * buckets,), jnp.int32),
            pltpu.VMEM((NOTE, wide), F32),
            pltpu.SemaphoreType.DMA((2 * CAPC,)),
        ],
        cost_estimate=pl.CostEstimate(flops=0, bytes_accessed=8 * CAPC * high * wide, transcendentals=0),
        name="take_leads",
    )(dest, counts, offsets, tiles)


def gram_table(col_count):
    blocks = col_count
    table = []
    for c in range(col_count):
        low = min(c, blocks - 1 - c)
        shared = [(i, j) for i in (low, blocks - 1 - low) for j in range(i, blocks)]
        mine = shared[::2] if c == low else shared[1::2]
        table.append((mine + mine[-1:])[: GRAM_SLOTS])
    return table


def place_leads(pos_ref, lead_refs, sum_ref, transposed):
    sum_ref[...] = jnp.zeros_like(sum_ref)
    count, size = lead_refs[0].shape[0], lead_refs[0].shape[2]
    for s, ref in enumerate(lead_refs):

        def place(r, _, s=s, ref=ref):
            pos = pos_ref[s * count + r]

            @pl.when(pos >= 0)
            def _():
                at_row = pl.ds(pl.multiple_of((pos // PANELS) * size, size), size)
                at_col = pl.ds(pl.multiple_of((pos % PANELS) * size, size), size)
                if transposed:
                    sum_ref[at_col, at_row] += ref[r, :size].T
                else:
                    sum_ref[at_row, at_col] += ref[r, :size]

            return 0

        lax.fori_loop(0, count, place, 0)


def gram_slice(mine, positions, leads):
    size = leads[0].shape[2]
    width, depth = PANELS * size, RTD * size

    def kernel(mine_ref, pos_ref, *refs):
        lead_refs, (out_ref, sum_ref, left_ref) = refs[: len(leads)], refs[len(leads) :]
        place_leads(pos_ref, lead_refs, sum_ref, False)

        def block(s, _):
            at_i = pl.ds(pl.multiple_of(mine_ref[2 * s] * BLK, BLK), BLK)
            at_j = pl.ds(pl.multiple_of(mine_ref[2 * s + 1] * BLK, BLK), BLK)
            at_s = pl.ds(pl.multiple_of(s * BLK, BLK), BLK)
            for k in range(RTD):
                rows = slice(k * size, (k + 1) * size)
                left_ref[:, rows] = sum_ref[rows, at_i].T
            a_high, a_low = split(left_ref[...])
            b_high, b_low = split(sum_ref[:, at_j])
            block_out = dot3(a_high, a_low, b_high, b_low)
            for g in range(BLK // 8):
                out_ref[g, :, at_s] = block_out[8 * g : 8 * g + 8]
            return 0

        lax.fori_loop(0, GRAM_SLOTS, block, 0)

    smem = pl.BlockSpec(memory_space=pltpu.SMEM)
    vmem = pl.BlockSpec(memory_space=pltpu.VMEM)
    return pl.pallas_call(
        kernel,
        in_specs=[smem, smem] + [vmem] * len(leads),
        out_specs=vmem,
        out_shape=jax.ShapeDtypeStruct((BLK // 8, 8, GRAM_SLOTS * BLK), F32),
        scratch_shapes=[pltpu.VMEM((depth, width), F32), pltpu.VMEM((BLK, depth), F32)],
        compiler_params=params(),
        cost_estimate=pl.CostEstimate(
            flops=6 * BLK * width * depth, bytes_accessed=4 * 16 * size * size, transcendentals=0
        ),
        name="gram_slice",
    )(mine, positions, *leads)


def leading_split(positions, leads):
    size = leads[0].shape[2]
    width, depth = PANELS * size, RTD * size

    def kernel(pos_ref, *refs):
        lead_refs, (high_ref, low_ref, sum_ref) = refs[: len(leads)], refs[len(leads) :]
        place_leads(pos_ref, lead_refs, sum_ref, True)

        def step(k, _):
            rows = pl.ds(pl.multiple_of(k * BLK, BLK), BLK)
            high_ref[rows, :], low_ref[rows, :] = split(sum_ref[rows, :])
            return 0

        lax.fori_loop(0, width // BLK, step, 0)

    smem = pl.BlockSpec(memory_space=pltpu.SMEM)
    vmem = pl.BlockSpec(memory_space=pltpu.VMEM)
    return pl.pallas_call(
        kernel,
        in_specs=[smem] + [vmem] * len(leads),
        out_specs=[vmem, vmem],
        out_shape=[jax.ShapeDtypeStruct((width, depth), BF16)] * 2,
        scratch_shapes=[pltpu.VMEM((width, depth), F32)],
        compiler_params=params(),
        cost_estimate=pl.CostEstimate(flops=0, bytes_accessed=12 << 20, transcendentals=0),
        name="leading_split",
    )(positions, *leads)


def cross_products(positions, groups, lead_high, lead_low):
    width, depth = lead_high.shape
    size = groups[0][0][0].shape[-2]
    chunks = len(groups[0][0])
    count = len(groups) * CAPC
    step = 256

    def kernel(pos_ref, *refs):
        tile_refs, (high_ref, low_ref, out_ref) = refs[: len(groups) * chunks], refs[len(groups) * chunks :]
        out_ref[...] = jnp.zeros_like(out_ref)
        for g in range(len(groups)):
            parts = tile_refs[g * chunks : (g + 1) * chunks]

            def place(i, _, parts=parts, first=g * CAPC):
                pos = pos_ref[first + i]

                @pl.when(pos >= 0)
                def _():
                    at_row = pl.ds(pl.multiple_of((pos // PANELS) * size, size), size)
                    at_col = pl.ds(pl.multiple_of((pos % PANELS) * size, size), size)
                    b_high, b_low = split(jnp.concatenate([ref[0, i] for ref in parts], axis=1))
                    dot = lambda x, y: jnp.dot(x, y, preferred_element_type=F32)
                    for m in range(0, width, step):
                        a_high, a_low = high_ref[m : m + step, at_row], low_ref[m : m + step, at_row]
                        out_ref[m : m + step, at_col] += dot(a_high, b_high) + dot(a_high, b_low) + dot(a_low, b_high)

                return 0

            lax.fori_loop(0, CAPC, place, 0)

    return pl.pallas_call(
        kernel,
        grid_spec=pltpu.PrefetchScalarGridSpec(
            num_scalar_prefetch=1,
            grid=(1,),
            in_specs=[
                pl.BlockSpec((1, *v.shape[1:]), lambda i, pos, n=n: (n, 0, 0, 0), pipeline_mode=pl.Buffered(1))
                for vs, n in groups
                for v in vs
            ]
            + [pl.BlockSpec((width, depth), lambda i, pos: (0, 0), pipeline_mode=pl.Buffered(1))] * 2,
            out_specs=pl.BlockSpec((width, PANELS * size), lambda i, pos: (0, 0), pipeline_mode=pl.Buffered(1)),
        ),
        out_shape=jax.ShapeDtypeStruct((width, PANELS * size), F32),
        compiler_params=params(),
        cost_estimate=pl.CostEstimate(
            flops=6 * count * width * size * size, bytes_accessed=16 << 20, transcendentals=0
        ),
        name="cross_products",
    )(positions, *[v for vs, _ in groups for v in vs], lead_high, lead_low)


def block_factor(block):
    tiles = BLK // 8
    lane = lax.broadcasted_iota(jnp.int32, (8, BLK), 1)
    sub = lax.broadcasted_iota(jnp.int32, (8, BLK), 0)
    full = lambda v: jnp.broadcast_to(v, (8, BLK))
    x = [block[8 * t : 8 * t + 8, :] for t in range(tiles)]
    out = []
    for t in range(tiles):
        base = 8 * t
        panel = lane // 8 == t
        rows = [full(x[t][p : p + 1, :]) for p in range(8)]
        a = {(p, q): full(rows[p][:, base + q : base + q + 1]) for p in range(8) for q in range(p, 8)}
        rows = [jnp.where(panel, jnp.where(lane == base + p, 1.0, 0.0), rows[p]) for p in range(8)]
        columns = {u: [full(x[u][:, base + p : base + p + 1]) for p in range(8)] for u in range(t + 1, tiles)}
        for u in range(t + 1, tiles):
            x[u] = jnp.where(panel, 0.0, x[u])
        scales = []
        for p in range(8):
            inverse = 1.0 / a[p, p]
            scale = lax.rsqrt(a[p, p])
            scales.append(scale * (1.5 - 0.5 * a[p, p] * scale * scale))
            scaled = rows[p] * inverse
            ratio = [a[p, q] * inverse for q in range(p + 1, 8)]
            for q in range(p + 1, 8):
                for r in range(q, 8):
                    a[q, r] = a[q, r] - a[p, q] * ratio[r - p - 1]
                rows[q] = rows[q] - a[p, q] * scaled
            for u in range(t + 1, tiles):
                for q in range(p + 1, 8):
                    columns[u][q] = columns[u][q] - columns[u][p] * ratio[q - p - 1]
                x[u] = x[u] - columns[u][p] * scaled
        tile = rows[0] * scales[0]
        for p in range(1, 8):
            tile = jnp.where(sub == p, rows[p] * scales[p], tile)
        out.append(jnp.where(lane <= sub + base, tile, 0.0))
    return jnp.concatenate(out, axis=0)


def eliminate(first, last, work_ref, out_ref, row_ref):
    width = work_ref.shape[1]

    def outer(k, _):
        at = pl.multiple_of(k * BLK, BLK)
        here = pl.ds(at, BLK)
        inverse = block_factor(work_ref[here, here])
        row_ref[...] = jnp.dot(inverse, work_ref[here, :], precision=HIGHEST, preferred_element_type=F32)
        row_ref[:, here] = inverse
        row = row_ref[...]
        lane = lax.broadcasted_iota(jnp.int32, (BLK, width), 1)
        out_ref[pl.ds(pl.multiple_of(at - first * BLK, BLK), BLK), :] = jnp.where(lane < at + BLK, row, 0.0)

        def inner(i, _):
            below = pl.ds(pl.multiple_of(i * BLK, BLK), BLK)
            factor = row_ref[:, below].T
            work_ref[below, here] = jnp.zeros((BLK, BLK), F32)
            work_ref[below, :] -= jnp.dot(factor, row, precision=HIGHEST, preferred_element_type=F32)
            return 0

        lax.fori_loop(k + 1, width // BLK, inner, 0)
        return 0

    lax.fori_loop(first, last, outer, 0)


def inverse_cholesky_start(spots, parts, width):
    def kernel(spot_ref, *refs):
        part_refs, (out_ref, rest_ref, work_ref, row_ref) = refs[: len(parts)], refs[len(parts) :]
        for n, ref in enumerate(part_refs):
            count = ref.shape[0]

            def fill(s, _, n=n, ref=ref, count=count):
                q, r = s // GRAM_SLOTS, s % GRAM_SLOTS
                at = 2 * (n * count * GRAM_SLOTS + s)
                row = pl.multiple_of(spot_ref[at] * BLK, BLK)
                col = pl.multiple_of(spot_ref[at + 1] * BLK, BLK)
                lanes = pl.ds(pl.multiple_of(r * BLK, BLK), BLK)
                for g in range(BLK // 8):
                    work_ref[pl.ds(row + 8 * g, 8), pl.ds(col, BLK)] = ref[q, g, :, lanes]
                return 0

            lax.fori_loop(0, count * GRAM_SLOTS, fill, 0)
        eliminate(0, FIRST, work_ref, out_ref, row_ref)
        rest_ref[...] = work_ref[FIRST * BLK :, :]

    smem = pl.BlockSpec(memory_space=pltpu.SMEM)
    vmem = pl.BlockSpec(memory_space=pltpu.VMEM)
    return pl.pallas_call(
        kernel,
        in_specs=[smem] + [vmem] * len(parts),
        out_specs=[vmem, vmem],
        out_shape=[
            jax.ShapeDtypeStruct((FIRST * BLK, width), F32),
            jax.ShapeDtypeStruct((width - FIRST * BLK, width), F32),
        ],
        scratch_shapes=[pltpu.VMEM((width, width), F32), pltpu.VMEM((BLK, width), F32)],
        compiler_params=params(),
        cost_estimate=pl.CostEstimate(flops=CHOL_COST, bytes_accessed=8 << 20, transcendentals=0),
        name="inverse_cholesky_start",
    )(spots, *parts)


def inverse_cholesky_end(rest):
    low, width = rest.shape
    first = (width - low) // BLK

    def kernel(rest_ref, out_ref, work_ref, row_ref):
        work_ref[first * BLK :, :] = rest_ref[...]
        eliminate(first, width // BLK, work_ref, out_ref, row_ref)

    vmem = pl.BlockSpec(memory_space=pltpu.VMEM)
    return pl.pallas_call(
        kernel,
        in_specs=[vmem],
        out_specs=vmem,
        out_shape=jax.ShapeDtypeStruct((low, width), F32),
        scratch_shapes=[pltpu.VMEM((width, width), F32), pltpu.VMEM((BLK, width), F32)],
        compiler_params=params(),
        cost_estimate=pl.CostEstimate(flops=CHOL_COST, bytes_accessed=8 << 20, transcendentals=0),
        name="inverse_cholesky_end",
    )(rest)


def solved_rows(col_here, inverses, crosses):
    width, cols = crosses[0].shape[0], sum(c.shape[1] for c in crosses)
    wide = crosses[0].shape[1] // PANELS
    size = wide * len(crosses)

    def kernel(col_ref, *refs):
        inv_refs, refs = refs[: len(inverses)], refs[len(inverses) :]
        cross_refs, (out_ref, high_ref, low_ref) = refs[: len(crosses)], refs[len(crosses) :]
        i = pl.program_id(0)

        @pl.when(i == 0)
        def _():
            at = 0
            for ref in inv_refs:
                rows = slice(at, at + ref.shape[0])
                high_ref[rows, :], low_ref[rows, :] = split(ref[...])
                at += ref.shape[0]

        b_high, b_low = split(jnp.concatenate([ref[...] for ref in cross_refs], axis=1))
        first = col_ref[0] * cols + i * size
        step = 256
        for k in range(width // step):
            rows, done = slice(k * step, (k + 1) * step), (k + 1) * step
            value = dot3(high_ref[rows, :done], low_ref[rows, :done], b_high[:done], b_low[:done])
            row = lax.broadcasted_iota(jnp.int32, (step, size), 0) + k * step
            col = lax.broadcasted_iota(jnp.int32, (step, size), 1) + first
            out_ref[rows, :] = jnp.where(col >= row, value, 0.0)

    return pl.pallas_call(
        kernel,
        grid_spec=pltpu.PrefetchScalarGridSpec(
            num_scalar_prefetch=1,
            grid=(cols // size,),
            in_specs=[
                pl.BlockSpec(part.shape, lambda i, col: (0, 0), pipeline_mode=pl.Buffered(1)) for part in inverses
            ]
            + [pl.BlockSpec((width, wide), lambda i, col: (0, i))] * len(crosses),
            out_specs=pl.BlockSpec((width, size), lambda i, col: (0, i)),
            scratch_shapes=[pltpu.VMEM((width, width), BF16)] * 2,
        ),
        out_shape=jax.ShapeDtypeStruct((width, cols), F32),
        compiler_params=params(),
        cost_estimate=pl.CostEstimate(flops=6 * width * width * cols, bytes_accessed=12 << 20, transcendentals=0),
        name="solved_rows",
    )(col_here, *inverses, *crosses)


def rotated(amount, value, row_count):
    def by(shift):
        if shift == 0:
            return lambda v: v
        pairs = [(i, (i + shift) % row_count) for i in range(row_count)]
        return lambda v: lax.ppermute(v, "row", pairs)

    return lax.switch(amount, [by(k) for k in range(row_count)], value)


def step_pairs(step, col_count):
    half = col_count // 2
    return [(i, ((i // 2 + step) % half) * 2 + i % 2) for i in range(col_count)]


def pair_steps(value, col_count):
    return [value] + [lax.ppermute(value, "col", step_pairs(d, col_count)) for d in range(1, col_count // 2)]


def both_cores(own, col_count):
    own = jnp.stack(own)
    return own, lax.ppermute(own, "col", [(i, i ^ 1) for i in range(col_count)])


def exchanged(parts, axis):
    return lax.all_to_all(parts, axis, split_axis=0, concat_axis=0, tiled=True)


def repeated_sum(parts):
    count, rows, wide = parts.shape
    block = pl.BlockSpec((count, 8, wide), lambda i: (0, i, 0))

    def kernel(in_ref, out_ref):
        out_ref[...] = jnp.broadcast_to(jnp.sum(in_ref[...], axis=0)[None], out_ref.shape)

    return pl.pallas_call(
        kernel,
        grid=(rows // 8,),
        in_specs=[block],
        out_specs=block,
        out_shape=jax.ShapeDtypeStruct(parts.shape, F32),
        cost_estimate=pl.CostEstimate(flops=count * rows * wide, bytes_accessed=8 * count * rows * wide, transcendentals=0),
        name="repeated_sum",
    )(parts)


def summed_rows(parts):
    return exchanged(repeated_sum(exchanged(parts, "row")), "row")


def shards(child_tiles, tile_dest, tile_counts, child_offsets):
    row_count = lax.axis_size("row")
    col_count = lax.axis_size("col")
    col_here = lax.axis_index("col")
    size = child_tiles.shape[1]
    width = PANELS * size
    cols = jnp.arange(col_count, dtype=jnp.int32)
    child_of = cols // (col_count // CHILDREN)
    offsets = jnp.sum(jnp.where(child_of[:, None] == jnp.arange(CHILDREN)[None, :], child_offsets[None, :], 0), axis=1)
    offset_here = jnp.sum(jnp.where(cols == col_here, offsets, 0))
    amount = offset_here % row_count

    taken = take_leads(child_tiles, tile_dest, tile_counts, child_offsets, col_count, row_count)
    lead = rotated(amount, taken, row_count)
    near = pair_steps(lead, col_count)
    my_picks = lead[0, size, : col_count * CAPC].astype(jnp.int32).reshape(col_count, CAPC)
    half = col_count // 2
    steps = jnp.arange(half)[:, None]
    targets = ((col_here // 2 + steps) % half) * 2 + (col_here + jnp.arange(2)[None, :]) % 2
    chosen = targets[:, :, None] == cols
    my_picks = jnp.sum(jnp.where(chosen[..., None], my_picks, 0), axis=2).reshape(half, 2 * CAPC)
    wide = size // CHUNKS
    far, stacks = [], None
    for c in range(CHUNKS):
        ready = child_tiles[:, :, c * wide : (c + 1) * wide]
        if c == 0:
            ready, _, my_picks = lax.optimization_barrier((ready, lead, my_picks))
        else:
            ready, _, _ = lax.optimization_barrier((ready, packed, stacks[0]))
        tiles = rotated(amount, ready, row_count)
        if c == 0:
            near, tiles = lax.optimization_barrier((near, tiles))
            stacks = both_cores(near, col_count)
        else:
            far, tiles = lax.optimization_barrier((far, tiles))
        packed = [v.reshape(2, CAPC, size, wide) for v in take_groups(tiles, my_picks)]
        if c == CHUNKS - 1:
            stacks, packed = lax.optimization_barrier((stacks, packed))
        far.append([packed[0]] + [lax.ppermute(packed[d], "col", step_pairs(d, col_count)) for d in range(1, half)])

    notes = jnp.concatenate([v[:, 0, size, : 2 * col_count * CAPC] for v in stacks]).astype(jnp.int32)
    places = notes[:, col_count * CAPC :].reshape(col_count, col_count, CAPC)
    lead_places = places[:, 0].reshape(-1)
    order = jnp.stack([((col_here // 2 - d) % half) * 2 + (col_here + c) % 2 for c in range(2) for d in range(half)])
    ordered = order[:, None] == cols[None, :]
    my_places = jnp.sum(jnp.where(cols[None, :, None] == col_here, places, 0), axis=1).reshape(-1)
    table = jnp.array(gram_table(col_count), jnp.int32).reshape(col_count, -1)
    spots = jnp.sum(jnp.where(ordered[:, :, None], table[None], 0), axis=1)
    col_scalar = col_here.reshape(1).astype(jnp.int32)

    leads = [v.reshape(-1, *v.shape[2:]) for v in stacks]
    gram_part = summed_rows(gram_slice(spots[0], lead_places, leads))
    swap = [(i, i ^ 1) for i in range(col_count)]
    lead_high, lead_low = leading_split(lead_places, leads)
    others = [[lax.ppermute(v, "col", swap) for v in chunk] for chunk in far[:-1]]
    far, gram_part, lead_high, lead_low = lax.optimization_barrier((far, gram_part, lead_high, lead_low))
    others.append([lax.ppermute(v, "col", swap) for v in far[-1]])
    others, gram_part = lax.optimization_barrier((others, gram_part))
    gram_near = pair_steps(gram_part, col_count)
    groups = [(v, 0) for v in zip(*far)] + [(v, 1) for v in zip(*others)]
    cross = cross_products(my_places, groups, lead_high, lead_low)
    gram_near, cross = lax.optimization_barrier((gram_near, cross))
    gram_parts, cross = lax.optimization_barrier((both_cores(gram_near, col_count), cross))
    cross = summed_rows(cross.reshape(row_count, width // row_count, -1)).reshape(width, -1)
    begun, rest = inverse_cholesky_start(spots.reshape(-1), gram_parts, width)
    ended = inverse_cholesky_end(rest)
    return solved_rows(col_scalar, [begun, ended], [cross])


def solution(mesh):
    return jax.shard_map(
        shards,
        mesh=mesh,
        in_specs=(P(("row", "col"), None, None), P(("row", "col"), None), P("row", "col"), P()),
        out_specs=P(None, "col"),
        check_vma=False,
    )
```
